768 devices in a mesh: shard: 96 (over z, x, y_lo), grp: 8 (over y_hi, core).
Axes of the slice: x: 4, y: 8 (y_hi: 4, y_lo: 2; y = y_hi * 2 + y_lo), z: 12, core: 2. Of those that a mesh axis runs over, the one named last changes fastest.
Arguments:
- embeddings: bfloat16 [196608, 1024], P('shard', 'grp')
- clusters: int32 [196608], P('shard'), may hold values from 0 to 3, as said below
- blocks: int32 [768, 4], P('shard'), may hold values from 0 to 767, as said below
- counts: int32 [768], P('shard'), may hold values from 1 to 4
- seed_mask: int32 [196608], P(('shard', 'grp')), may hold values 0 or 1
- prior: bfloat16 [196608, 256], P(('shard', 'grp')), may hold values from 0 to 1
Outputs:
- labels: bfloat16 [196608, 256], P(('shard', 'grp'))
The draws below stay inside these ranges and needn't reach their ends.
Inputs may be any that keep to these rules, and one draw needn't show every extreme that they name: `blocks`: slot 0 of row tile r is r itself; the other slots hold distinct tiles of the same shard or of the first 2 tiles of the next shard, never past the last tile; slots at or past counts hold such tiles too but carry no affinity. `clusters`: images 2m and 2m + 1 share a cluster.
All inputs are finite; a program needn't handle non-finite values. No bound on the sum of `seed_mask` on one device may be relied on, other than what follows from the above.
Results may differ from the reference program's by a relative error of at most 0.0038.
Values may be sent and summed in bfloat16 or wider, within the bound.
A program may use at most 32 MiB of HBM per device.

```python
import jax
import jax.numpy as jnp
from jax import lax

D = 1024
C = 256
TILE = 256
K = 4
CLUSTERS = 4
STEPS = 2
TPS = 8
ROW_TILES = 768
IMAGES = 196608
WINDOW = 10


def draw_embeddings(key, part):
    first = jax.random.fold_in(key, 0)
    values = jnp.clip(jax.random.normal(first, (IMAGES, D), jnp.float32), -6.0, 6.0)
    return (values / jnp.sqrt(jnp.float32(D))).astype(jnp.bfloat16)


def draw_clusters(key, part):
    paired = jax.random.randint(key, (IMAGES // 2,), 0, CLUSTERS)
    return jnp.repeat(paired, 2).astype(jnp.int32)


def draw_blocks(key, part):
    rows = jnp.arange(ROW_TILES, dtype=jnp.int32)
    base = rows // TPS * TPS
    offsets = jnp.arange(WINDOW, dtype=jnp.int32)
    candidates = base[:, None] + offsets[None, :]
    usable = (candidates < ROW_TILES) & (candidates != rows[:, None])
    scores = jax.random.randint(key, (ROW_TILES, WINDOW), 0, 1 << 20) * WINDOW + offsets[None, :]
    scores = jnp.where(usable, scores, 1 << 30)
    order = jnp.argsort(scores, axis=1, stable=True)
    picked = jnp.take_along_axis(candidates, order[:, :K - 1], axis=1)
    return jnp.concatenate([rows[:, None], picked], axis=1).astype(jnp.int32)


def place_ends(entries, key, low, high):
    place = [jax.random.randint(jax.random.fold_in(key, axis), (), 0, length) for axis, length in enumerate(entries.shape)]
    widest = entries.shape.index(max(entries.shape))
    neighbour = place[:widest] + [(place[widest] + 1) % entries.shape[widest]] + place[widest + 1:]
    return entries.at[tuple(place)].set(low).at[tuple(neighbour)].set(high)


def levels(rng, extent, cuts, smallest, largest):
    def one(dim, parts):
        heights = jax.random.uniform(jax.random.fold_in(jax.random.fold_in(rng, 6), dim), (parts,), jnp.float32, smallest / len(cuts), largest / len(cuts))
        return jnp.repeat(jnp.exp(heights), extent[dim] // parts).reshape((-1,) + (1,) * (len(extent) - dim - 1))

    gain = one(*cuts[0])
    for cut in cuts[1:]:
        gain = gain * one(*cut)
    return gain


def setup_inputs(seed: int = 0) -> dict:
    arg_keys = jax.random.split(jax.random.key(seed), 7)
    return {
        "embeddings": draw_embeddings(jax.random.fold_in(arg_keys[6], 71), 0),
        "clusters": draw_clusters(jax.random.fold_in(arg_keys[6], 71), 0),
        "blocks": draw_blocks(jax.random.fold_in(arg_keys[6], 71), 0),
        "counts": place_ends(jax.random.randint(arg_keys[3], (ROW_TILES,), 1, K + 1), jax.random.fold_in(arg_keys[3], 1), 1, K).astype(jnp.int32),
        "seed_mask": place_ends((jax.random.randint(arg_keys[4], (IMAGES,), 0, 4) < 1).astype(jnp.int32), jax.random.fold_in(arg_keys[4], 1), 0, 1),
        "prior": jnp.clip(1.0 * jax.random.uniform(arg_keys[5], (IMAGES, C), jnp.float32) ** levels(arg_keys[5], (IMAGES, C), ((0, 768),), -0.2, 0.2), 0.0, 1.0).astype(jnp.bfloat16),
    }


kernel_width = 0.06
spread_weight = 0.6


def reference(embeddings, clusters, blocks, counts, seed_mask, prior):
    tiles_x = embeddings.reshape(ROW_TILES, TILE, D)
    norms = jnp.sum(jnp.square(embeddings.astype(jnp.float32)), axis=-1).reshape(ROW_TILES, TILE)
    tiles_c = clusters.reshape(ROW_TILES, TILE)
    slot_index = jnp.arange(K, dtype=jnp.int32)
    image_index = jnp.arange(TILE, dtype=jnp.int32)

    def affinity_of(row):
        ids = blocks[row]
        rows_x = tiles_x[row].astype(jnp.float32)
        cols_x = tiles_x[ids].astype(jnp.float32)
        dots = jnp.einsum("if,kjf->ikj", rows_x, cols_x, precision=lax.Precision.HIGHEST)
        dist = norms[row][:, None, None] + norms[ids][None, :, :] - 2.0 * dots
        live = slot_index < counts[row]
        same = tiles_c[row][:, None, None] == tiles_c[ids][None, :, :]
        itself = (ids[None, :, None] == row) & (image_index[:, None, None] == image_index[None, None, :])
        allowed = same & live[None, :, None] & jnp.logical_not(itself)
        logits = -dist / kernel_width
        top = jnp.max(jnp.where(allowed, logits, jnp.float32(-1e30)), axis=(1, 2), keepdims=True)
        weights = jnp.where(allowed, jnp.exp(logits - top), jnp.float32(0.0))
        total = jnp.sum(weights, axis=(1, 2), keepdims=True)
        return (weights / total).astype(jnp.bfloat16)

    all_rows = jnp.arange(ROW_TILES, dtype=jnp.int32)
    affinity = lax.map(affinity_of, all_rows)
    seeds = (seed_mask.astype(jnp.float32)[:, None] * prior.astype(jnp.float32)).reshape(ROW_TILES, TILE, C)
    labels = seeds.astype(jnp.bfloat16)
    for step in range(STEPS):
        current = labels

        def spread_of(row):
            picked = current[blocks[row]].astype(jnp.float32)
            spread = jnp.einsum("ikj,kjc->ic", affinity[row].astype(jnp.float32), picked, precision=lax.Precision.HIGHEST)
            return (spread_weight * spread + (1.0 - spread_weight) * seeds[row]).astype(jnp.bfloat16)

        labels = lax.map(spread_of, all_rows)
    return labels.reshape(IMAGES, C)
```

```python
import jax
import jax.numpy as jnp
from jax import lax
from jax.experimental import pallas as pl
from jax.experimental.pallas import tpu as pltpu
from jax.sharding import PartitionSpec as P

TILE = 256
K = 4
SPILL = 2
STEPS = 2
kernel_width = 0.06
spread_weight = 0.6

MESH = pl.DeviceIdType.MESH
CH = 4
PT = 2
FAR = 3.0e38
RB = 32
NT = (((1,), (1,)), ((), ()))


def kernel(emb, clu, blk, cnt, msk, pri, out,
           x0, x1, x2, x3, relay, sd, cs, l0, l1, gram, aff, nj, cl, res,
           lsem, rx, fx, rsp, fsp, rsd, fsd, rcs, rrl, rl1, rl1s, ro,
           sx, ssp, ssd, scs, srl, sfx, sfsp, sfsd, sl1, sl1s, so):
    xs = (x0, x1, x2, x3)
    shards = lax.axis_size("shard")
    s = lax.axis_index("shard")
    g = lax.axis_index("grp")
    a = g % 2
    h = g // 2
    c = (s % 2) * 2
    rel = (h + 4 - c) % 4
    cp = 2 - c
    relp = (h + 4 - cp) % 4
    centre = {"grp": 2 * c + a}
    partner = {"grp": 2 * h + 1 - a}
    above = {"shard": s - 1, "grp": 2 * cp + a}
    has_prev = s > 0
    has_next = s < shards - 1
    is_centre = rel == 0

    def member(d):
        return {"grp": 2 * ((c + d) % 4) + a}

    def rcopy(src, dst, ssem, rsem, dev):
        return pltpu.make_async_remote_copy(
            src_ref=src, dst_ref=dst, send_sem=ssem, recv_sem=rsem, device_id=dev, device_id_type=MESH)

    def arrived(ref, sem):
        pltpu.make_async_copy(ref, ref, sem).wait()

    bar = pltpu.get_barrier_semaphore()

    def greet(dev):
        pl.semaphore_signal(bar, inc=1, device_id=dev, device_id_type=MESH)

    @pl.when(is_centre)
    def _():
        for d in (1, 2, 3):
            greet(member(d))
        greet(partner)

        @pl.when(has_next)
        def _():
            for hh in range(4):
                greet({"shard": s + 1, "grp": 2 * hh + a})

    @pl.when(jnp.logical_not(is_centre))
    def _():
        greet(centre)

        @pl.when(rel != 2)
        def _():
            greet(member(2))

    @pl.when(is_centre)
    def _():
        pltpu.make_async_copy(emb, x0.at[a, pl.ds(0, 8)], lsem.at[0]).start()

    lane = lax.broadcasted_iota(jnp.int32, (1, TILE), 1)
    rowid = lax.broadcasted_iota(jnp.int32, (TILE, 1), 0)
    eye = rowid == lane

    def wide(ref, t):
        return jnp.concatenate([ref[2 * t:2 * t + 1, :], ref[2 * t + 1:2 * t + 2, :]], axis=1)

    mask_row = wide(msk, 0).astype(jnp.float32)
    pick = jnp.where(eye, mask_row, 0.0).astype(jnp.bfloat16)
    sd[...] = jnp.dot(pick, pri[...], preferred_element_type=jnp.float32).astype(jnp.bfloat16)

    @pl.when(is_centre & jnp.logical_not(has_next))
    def _():
        for x in xs:
            x[:, 8:10] = jnp.zeros((2, SPILL, TILE, 128), jnp.bfloat16)
        l0[8:10] = jnp.zeros((SPILL, TILE, TILE), jnp.bfloat16)
        l1[8:10] = jnp.zeros((SPILL, TILE, TILE), jnp.bfloat16)
        cs[...] = jnp.zeros((8, 128), jnp.int32)

    base = has_prev.astype(jnp.int32)

    @pl.when(is_centre)
    def _():
        pl.semaphore_wait(bar, 4 + base)

    @pl.when(jnp.logical_not(is_centre))
    def _():
        pl.semaphore_wait(bar, 1 + base + jnp.where(rel == 2, 2, 0))

    def rows(q):
        return pl.ds(q * PT, PT)

    def own_chunk(d, q):
        return rcopy(emb.at[rows(q)], xs[d].at[a, rows(q)], sx.at[q], rx.at[d, q], centre)

    def to_relay(q):
        via = member(3) if q < CH // 2 else member(1)
        return rcopy(emb.at[rows(q)], relay.at[rows(q % 2)], sx.at[q], rrl.at[q % 2], via)

    def from_relay(q):
        return rcopy(relay.at[rows(q % 2)], x2.at[a, rows(q)], srl.at[q % 2], rx.at[2, q], centre)

    def own_seed(d):
        return rcopy(sd, l0.at[g], ssd.at[0], rsd.at[d], centre)

    def spill_x(d):
        return rcopy(emb.at[pl.ds(0, SPILL)], xs[d].at[a, pl.ds(8, SPILL)], ssp.at[0], rsp.at[d], above)

    def spill_seed():
        return rcopy(sd, l0.at[8 + a], ssd.at[1], rsd.at[4], above)

    def spill_clu():
        return rcopy(clu.at[pl.ds(0, 8)], cs, scs.at[0], rcs.at[0], above)

    for d in (1, 3):
        @pl.when(rel == d)
        def _(d=d):
            for q in range(CH):
                own_chunk(d, q).start()
            own_seed(d).start()

    @pl.when(rel == 2)
    def _():
        for q in (0, 2, 1, 3):
            to_relay(q).start()
        own_seed(2).start()

    def own_x(q):
        return rcopy(emb.at[rows(q)], x0.at[a, rows(q)], sfx.at[0, q], fx.at[0, q], partner)

    def own_l():
        return rcopy(sd, l0.at[g], ssd.at[0], fsd.at[0], partner)

    @pl.when(is_centre)
    def _():
        for q in range(CH):
            own_x(q).start()
        own_l().start()

    for d in range(4):
        @pl.when(has_prev & (relp == d))
        def _(d=d):
            spill_x(d).start()

    @pl.when(has_prev & (h == 0))
    def _():
        spill_clu().start()
        spill_seed().start()

    for d, first in ((3, 0), (1, 2)):
        @pl.when(rel == d)
        def _(d=d, first=first):
            for q in (first, first + 1):
                arrived(relay.at[rows(q % 2)], rrl.at[q % 2])
                from_relay(q).start()

    def fwd_x(d, q):
        return rcopy(xs[d].at[a, rows(q)], xs[d].at[a, rows(q)], sfx.at[d, q], fx.at[d, q], partner)

    def fwd_sp(d):
        return rcopy(xs[d].at[a, pl.ds(8, SPILL)], xs[d].at[a, pl.ds(8, SPILL)], sfsp.at[d], fsp.at[d], partner)

    def seed_tile(d):
        return 2 * ((c + d) % 4) + a if d < 4 else 8 + a

    def fwd_seed(d):
        t = seed_tile(d)
        return rcopy(l0.at[t], l0.at[t], sfsd.at[d], fsd.at[d], partner)

    def send_l1(j):
        r = 2 * j + a
        return rcopy(l1.at[r], l1.at[r], sl1.at[j], rl1.at[j], partner)

    def spill_l1():
        return rcopy(l1.at[a], l1.at[8 + a], sl1s.at[0], rl1s.at[0], above)

    def fwd_l1():
        return rcopy(l1.at[8 + a], l1.at[8 + a], sl1s.at[1], rl1s.at[1], partner)

    def result(j):
        return rcopy(res.at[j], out, so.at[j], ro.at[0], {"grp": 2 * j + a})

    def own_result(j):
        return pltpu.make_async_copy(res.at[j], out, lsem.at[1])

    def pair(x, t):
        return jnp.concatenate([x[0, t], x[1, t]], axis=1)

    def tile_of(r, k):
        return jnp.clip(blk[r, k] - 8 * s, 0, 8 + SPILL - 1)

    def norms(d, lo, hi):
        ones = jnp.ones((8, TILE), jnp.bfloat16)

        def body(t, carry):
            v = pair(xs[d], t).astype(jnp.float32)
            sq = v * v
            big = sq.astype(jnp.bfloat16)
            small = (sq - big.astype(jnp.float32)).astype(jnp.bfloat16)
            n = lax.dot_general(ones, big, NT, preferred_element_type=jnp.float32)
            n += lax.dot_general(ones, small, NT, preferred_element_type=jnp.float32)
            nj[t] = n if d == 0 else nj[t] + n
            return carry

        lax.fori_loop(lo, hi, body, 0)

    def products(d):
        def body(j, carry):
            r = 2 * j + a
            left = pair(xs[d], r)
            for k in range(K):
                right = pair(xs[d], tile_of(r, k))
                v = lax.dot_general(left, right, NT, preferred_element_type=jnp.float32)
                at = (j, slice(None), slice(k * TILE, (k + 1) * TILE))
                gram[at] = v if d == 0 else gram[at] + v
            return carry

        lax.fori_loop(0, 4, body, 0)

    def column(row):
        return jnp.sum(jnp.where(eye, row, 0.0), axis=1, keepdims=True)

    def softmax(j, carry):
        r = 2 * j + a
        n_i = column(nj[r][0:1, :])
        c_i = column(cl[r][0:1, :])
        n_j, c_j, self_id = [], [], []
        for k in range(K):
            t = tile_of(r, k)
            n_j.append(nj[t][0:1, :])
            c_j.append(jnp.where(k < cnt[r], cl[t][0:1, :], -1.0))
            self_id.append(jnp.where(t == r, rowid, -1))
        for b in range(TILE // RB):
            rs = slice(b * RB, (b + 1) * RB)
            dist = []
            for k in range(K):
                dot = gram[j, rs, k * TILE:(k + 1) * TILE]
                t = (n_i[rs] + n_j[k]) - 2.0 * dot
                ok = (c_i[rs] == c_j[k]) & (self_id[k][rs] != lane)
                dist.append(jnp.where(ok, t, FAR))
            low = jnp.minimum(jnp.minimum(dist[0], dist[1]), jnp.minimum(dist[2], dist[3]))
            near = jnp.min(low, axis=1, keepdims=True)
            w = [jnp.exp((near - t) * (1.0 / kernel_width)) for t in dist]
            total = jnp.sum((w[0] + w[1]) + (w[2] + w[3]), axis=1, keepdims=True)
            inv = 1.0 / total
            for k in range(K):
                aff[j, rs, k * TILE:(k + 1) * TILE] = (w[k] * inv).astype(jnp.bfloat16)
        return carry

    def spread(j, labels):
        r = 2 * j + a
        acc = None
        for k in range(K):
            part = jnp.dot(aff[j, :, k * TILE:(k + 1) * TILE], labels[tile_of(r, k)],
                           preferred_element_type=jnp.float32)
            acc = part if acc is None else acc + part
        seeds = l0[r].astype(jnp.float32)
        return (spread_weight * acc + (1.0 - spread_weight) * seeds).astype(jnp.bfloat16)

    @pl.when(is_centre)
    def _():
        l0[g] = sd[...]
        for t in range(8):
            cl[t] = jnp.broadcast_to(wide(clu, t).astype(jnp.float32), (8, TILE))
        pltpu.make_async_copy(emb, x0.at[a, pl.ds(0, 8)], lsem.at[0]).wait()
        for d in (1, 2, 3):
            arrived(l0.at[0], rsd.at[d])
            fwd_seed(d).start()

        @pl.when(has_next)
        def _():
            for d in range(4):
                arrived(x0.at[0, pl.ds(8, SPILL)], rsp.at[d])
                fwd_sp(d).start()
            arrived(l0.at[0], rsd.at[4])
            fwd_seed(4).start()
            arrived(cs, rcs.at[0])

        for t in range(2):
            cl[8 + t] = jnp.broadcast_to(wide(cs, t).astype(jnp.float32), (8, TILE))

        def here(d):
            for q in range(CH):
                arrived(x0.at[0, rows(0)], fx.at[d, q])

            @pl.when(has_next)
            def _():
                arrived(x0.at[0, pl.ds(8, SPILL)], fsp.at[d])

        here(0)
        norms(0, 0, 10)
        products(0)
        for q in range(CH):
            for d in (1, 3):
                arrived(x0.at[0, rows(0)], rx.at[d, q])
                fwd_x(d, q).start()
        for q in (0, 2):
            arrived(x0.at[0, rows(0)], rx.at[2, q])
            fwd_x(2, q).start()
        for d in (1, 3):
            here(d)
            norms(d, 0, 10)
            products(d)
        for q in (1, 3):
            arrived(x0.at[0, rows(0)], rx.at[2, q])
            fwd_x(2, q).start()
        here(2)
        norms(2, 0, 10)
        products(2)
        for d in range(4):
            arrived(l0.at[0], fsd.at[d])

        @pl.when(has_next)
        def _():
            arrived(l0.at[0], fsd.at[4])

        for j in range(4):
            softmax(j, 0)
            l1[2 * j + a] = spread(j, l0)
            send_l1(j).start()
            if j == 0:
                @pl.when(has_prev)
                def _():
                    spill_l1().start()

        @pl.when(has_next)
        def _():
            arrived(l1.at[0], rl1s.at[0])
            fwd_l1().start()

        for j in range(4):
            arrived(l1.at[0], rl1.at[j])

        @pl.when(has_next)
        def _():
            arrived(l1.at[0], rl1s.at[1])

        for j in range(4):
            res[j] = spread(j, l1)

            @pl.when(c == j)
            def _(j=j):
                own_result(j).start()

            @pl.when(c != j)
            def _(j=j):
                result(j).start()

        for j in range(4):
            send_l1(j).wait_send()

            @pl.when(c == j)
            def _(j=j):
                own_result(j).wait()

            @pl.when(c != j)
            def _(j=j):
                result(j).wait_send()
        own_l().wait_send()
        for q in range(CH):
            own_x(q).wait_send()
            for d in (1, 2, 3):
                fwd_x(d, q).wait_send()
        for d in (1, 2, 3):
            fwd_seed(d).wait_send()

        @pl.when(has_next)
        def _():
            for d in range(4):
                fwd_sp(d).wait_send()
            fwd_seed(4).wait_send()
            fwd_l1().wait_send()

        @pl.when(has_prev)
        def _():
            spill_l1().wait_send()

    for d in range(4):
        @pl.when(has_prev & (relp == d))
        def _(d=d):
            spill_x(d).wait_send()

    @pl.when(has_prev & (h == 0))
    def _():
        spill_clu().wait_send()
        spill_seed().wait_send()

    for d, first in ((3, 0), (1, 2)):
        @pl.when(rel == d)
        def _(d=d, first=first):
            for q in range(CH):
                own_chunk(d, q).wait_send()
            own_seed(d).wait_send()
            for q in (first, first + 1):
                from_relay(q).wait_send()

    @pl.when(rel == 2)
    def _():
        for q in range(CH):
            to_relay(q).wait_send()
        own_seed(2).wait_send()

    @pl.when(jnp.logical_not(is_centre))
    def _():
        arrived(out, ro.at[0])


def local(embeddings, clusters, blocks, counts, seed_mask, prior):
    bf16, f32, i32 = jnp.bfloat16, jnp.float32, jnp.int32
    vmem = pl.BlockSpec(memory_space=pltpu.VMEM)
    smem = pl.BlockSpec(memory_space=pltpu.SMEM)
    anyw = pl.BlockSpec(memory_space=pl.ANY)
    V, D = pltpu.VMEM, pltpu.SemaphoreType.DMA
    x = V((2, 10, TILE, 128), bf16)
    return pl.pallas_call(
        kernel,
        out_shape=jax.ShapeDtypeStruct((TILE, TILE), bf16),
        in_specs=[anyw, vmem, smem, smem, vmem, vmem],
        out_specs=anyw,
        scratch_shapes=[
            x, x, x, x,
            V((4, TILE, 128), bf16),
            V((TILE, TILE), bf16),
            V((8, 128), i32),
            V((10, TILE, TILE), bf16),
            V((10, TILE, TILE), bf16),
            V((4, TILE, K * TILE), f32),
            V((4, TILE, K * TILE), bf16),
            V((10, 8, TILE), f32),
            V((10, 8, TILE), f32),
            V((4, TILE, TILE), bf16),
            D((2,)), D((4, CH)), D((4, CH)), D((4,)), D((4,)), D((5,)), D((5,)), D((1,)), D((2,)),
            D((4,)), D((2,)), D((1,)),
            D((CH,)), D((1,)), D((2,)), D((1,)), D((2,)), D((4, CH)), D((4,)), D((5,)), D((4,)), D((2,)), D((4,)),
        ],
        compiler_params=pltpu.CompilerParams(
            collective_id=0, has_side_effects=True, vmem_limit_bytes=40 * 1024 * 1024),
        name="spread",
    )(embeddings.reshape(8, TILE, 128), clusters.reshape(16, 128), blocks, counts,
      seed_mask.reshape(2, 128), prior)


def solution(mesh):
    in_specs = (
        P("shard", "grp"),
        P("shard"),
        P("shard", None),
        P("shard"),
        P(("shard", "grp")),
        P(("shard", "grp"), None),
    )
    out_specs = P(("shard", "grp"), None)
    return jax.shard_map(local, mesh=mesh, in_specs=in_specs, out_specs=out_specs, check_vma=False)
```

```python
import jax
import jax.numpy as jnp
from jax import lax
from jax.experimental import pallas as pl
from jax.experimental.pallas import tpu as pltpu
from jax.sharding import PartitionSpec as P

TILE = 256
K = 4
SPILL = 2
STEPS = 2
kernel_width = 0.06
spread_weight = 0.6

MESH = pl.DeviceIdType.MESH
CH = 4
PT = 2
FAR = 3.0e38
RB = 32
NT = (((1,), (1,)), ((), ()))


def kernel(emb, clu, blk, cnt, msk, pri, out,
           x0, x1, x2, x3, relay, pv, sd, cs, l0, l1, gram, aff, nj, cl, res,
           lsem, rx, fx, rsp, fsp, rsd, fsd, rcs, rrl, rl1, rl1s, ro,
           sx, ssp, ssd, scs, srl, sfx, sfsp, sfsd, sl1, sl1s, so):
    xs = (x0, x1, x2, x3)
    shards = lax.axis_size("shard")
    s = lax.axis_index("shard")
    g = lax.axis_index("grp")
    a = g % 2
    h = g // 2

    def centre_of(shard):
        return (shard // 8 + (shard % 8) // 2 + 2 * (shard % 2)) % 4

    c = centre_of(s)
    rel = (h + 4 - c) % 4
    cp = centre_of((s + shards - 1) % shards)
    zup, zdown = (s + 8) % shards, (s + shards - 8) % shards
    relp = (h + 4 - cp) % 4
    centre = {"grp": 2 * c + a}
    partner = {"grp": 2 * h + 1 - a}
    above = {"shard": s - 1, "grp": 2 * cp + a}
    has_prev = s > 0
    has_next = s < shards - 1
    is_centre = rel == 0

    def member(d):
        return {"grp": 2 * ((c + d) % 4) + a}

    def rcopy(src, dst, ssem, rsem, dev):
        return pltpu.make_async_remote_copy(
            src_ref=src, dst_ref=dst, send_sem=ssem, recv_sem=rsem, device_id=dev, device_id_type=MESH)

    def arrived(ref, sem):
        pltpu.make_async_copy(ref, ref, sem).wait()

    pltpu.make_async_copy(pri, pv, lsem.at[1]).start()
    bar = pltpu.get_barrier_semaphore()

    def greet(dev):
        pl.semaphore_signal(bar, inc=1, device_id=dev, device_id_type=MESH)

    @pl.when(is_centre)
    def _():
        for d in (1, 2, 3):
            greet(member(d))
        greet(partner)
        for z in (zup, zdown):
            greet({"shard": z, "grp": 2 * centre_of(z) + a})
            greet({"shard": z, "grp": 2 * ((centre_of(z) + 2) % 4) + a})

        @pl.when(has_next)
        def _():
            for hh in range(4):
                greet({"shard": s + 1, "grp": 2 * hh + a})

    @pl.when(jnp.logical_not(is_centre))
    def _():
        greet(centre)

    @pl.when(is_centre)
    def _():
        pltpu.make_async_copy(emb, x0.at[a, pl.ds(0, 8)], lsem.at[0]).start()

    lane = lax.broadcasted_iota(jnp.int32, (1, TILE), 1)
    rowid = lax.broadcasted_iota(jnp.int32, (TILE, 1), 0)
    eye = rowid == lane

    def wide(ref, t):
        return jnp.concatenate([ref[2 * t:2 * t + 1, :], ref[2 * t + 1:2 * t + 2, :]], axis=1)

    own_prior = pltpu.make_async_copy(pri, pv, lsem.at[1])
    own_prior.wait()
    mask_row = wide(msk, 0).astype(jnp.float32)
    pick = jnp.where(eye, mask_row, 0.0).astype(jnp.bfloat16)
    sd[...] = jnp.dot(pick, pv[...], preferred_element_type=jnp.float32).astype(jnp.bfloat16)

    @pl.when(is_centre & jnp.logical_not(has_next))
    def _():
        for x in xs:
            x[:, 8:10] = jnp.zeros((2, SPILL, TILE, 128), jnp.bfloat16)
        l0[8:10] = jnp.zeros((SPILL, TILE, TILE), jnp.bfloat16)
        l1[8:10] = jnp.zeros((SPILL, TILE, TILE), jnp.bfloat16)
        cs[...] = jnp.zeros((8, 128), jnp.int32)

    base = has_prev.astype(jnp.int32)

    @pl.when(is_centre)
    def _():
        pl.semaphore_wait(bar, 6 + base)

    @pl.when(jnp.logical_not(is_centre))
    def _():
        pl.semaphore_wait(bar, 1 + base + jnp.where(rel == 2, 2, 0))

    def rows(q):
        return pl.ds(q * PT, PT)

    def own_chunk(d, q):
        return rcopy(emb.at[rows(q)], xs[d].at[a, rows(q)], sx.at[q], rx.at[d, q], centre)

    def to_relay(q):
        via = {"shard": zup, "grp": 2 * ((c + 1) % 4) + a} if q < 2 else {"shard": zdown, "grp": 2 * ((c + 3) % 4) + a}
        return rcopy(emb.at[rows(q)], relay.at[rows(q)], sx.at[q], rrl.at[q], via)

    def from_relay(q):
        z = zdown if q < 2 else zup
        return rcopy(relay.at[rows(q)], x2.at[a, rows(q)], srl.at[q], rx.at[2, q],
                     {"shard": z, "grp": 2 * centre_of(z) + a})

    def own_seed(d):
        return rcopy(sd, l0.at[g], ssd.at[0], rsd.at[d], centre)

    def spill_x(d):
        return rcopy(emb.at[pl.ds(0, SPILL)], xs[d].at[a, pl.ds(8, SPILL)], ssp.at[0], rsp.at[d], above)

    def spill_seed():
        return rcopy(sd, l0.at[8 + a], ssd.at[1], rsd.at[4], above)

    def spill_clu():
        return rcopy(clu.at[pl.ds(0, 8)], cs, scs.at[0], rcs.at[0], above)

    for d in (1, 3):
        @pl.when(rel == d)
        def _(d=d):
            for q in range(CH):
                own_chunk(d, q).start()
            own_seed(d).start()

    @pl.when(rel == 2)
    def _():
        for q in (0, 2, 1, 3):
            to_relay(q).start()
        own_seed(2).start()

    def own_x(q):
        return rcopy(emb.at[rows(q)], x0.at[a, rows(q)], sfx.at[0, q], fx.at[0, q], partner)

    def own_l():
        return rcopy(sd, l0.at[g], ssd.at[0], fsd.at[0], partner)

    @pl.when(is_centre)
    def _():
        for q in range(CH):
            own_x(q).start()
        own_l().start()

    for d in range(4):
        @pl.when(has_prev & (relp == d))
        def _(d=d):
            spill_x(d).start()

    @pl.when(has_prev & (h == 0))
    def _():
        spill_clu().start()
        spill_seed().start()

    def fwd_x(d, q):
        return rcopy(xs[d].at[a, rows(q)], xs[d].at[a, rows(q)], sfx.at[d, q], fx.at[d, q], partner)

    def fwd_sp(d):
        return rcopy(xs[d].at[a, pl.ds(8, SPILL)], xs[d].at[a, pl.ds(8, SPILL)], sfsp.at[d], fsp.at[d], partner)

    def seed_tile(d):
        return 2 * ((c + d) % 4) + a if d < 4 else 8 + a

    def fwd_seed(d):
        t = seed_tile(d)
        return rcopy(l0.at[t], l0.at[t], sfsd.at[d], fsd.at[d], partner)

    def send_l1(j):
        r = 2 * j + a
        return rcopy(l1.at[r], l1.at[r], sl1.at[j], rl1.at[j], partner)

    def spill_l1():
        return rcopy(l1.at[a], l1.at[8 + a], sl1s.at[0], rl1s.at[0], above)

    def fwd_l1():
        return rcopy(l1.at[8 + a], l1.at[8 + a], sl1s.at[1], rl1s.at[1], partner)

    def result(j):
        return rcopy(res.at[j], out, so.at[j], ro.at[0], {"grp": 2 * j + a})

    def own_result(j):
        return pltpu.make_async_copy(res.at[j], out, lsem.at[1])

    def pair(x, t):
        return jnp.concatenate([x[0, t], x[1, t]], axis=1)

    def tile_of(r, k):
        return jnp.clip(blk[k, r] - 8 * s, 0, 8 + SPILL - 1)

    def norms(d, lo, hi):
        ones = jnp.ones((8, TILE), jnp.bfloat16)

        def body(t, carry):
            v = pair(xs[d], t).astype(jnp.float32)
            sq = v * v
            big = sq.astype(jnp.bfloat16)
            small = (sq - big.astype(jnp.float32)).astype(jnp.bfloat16)
            n = lax.dot_general(ones, big, NT, preferred_element_type=jnp.float32)
            n += lax.dot_general(ones, small, NT, preferred_element_type=jnp.float32)
            nj[t] = n if d == 0 else nj[t] + n
            return carry

        lax.fori_loop(lo, hi, body, 0)

    def products(d):
        def body(j, carry):
            r = 2 * j + a
            left = pair(xs[d], r)
            for k in range(K):
                right = pair(xs[d], tile_of(r, k))
                v = lax.dot_general(left, right, NT, preferred_element_type=jnp.float32)
                at = (j, slice(None), slice(k * TILE, (k + 1) * TILE))
                gram[at] = v if d == 0 else gram[at] + v
            return carry

        lax.fori_loop(0, 4, body, 0)

    def column(row):
        return jnp.sum(jnp.where(eye, row, 0.0), axis=1, keepdims=True)

    def softmax(j, carry):
        r = 2 * j + a
        n_i = column(nj[r][0:1, :])
        c_i = column(cl[r][0:1, :])
        n_j, c_j, self_id = [], [], []
        for k in range(K):
            t = tile_of(r, k)
            n_j.append(nj[t][0:1, :])
            c_j.append(jnp.where(k < cnt[r], cl[t][0:1, :], -1.0))
            self_id.append(jnp.where(t == r, rowid, -1))
        for b in range(TILE // RB):
            rs = slice(b * RB, (b + 1) * RB)
            dist = []
            for k in range(K):
                dot = gram[j, rs, k * TILE:(k + 1) * TILE]
                t = (n_i[rs] + n_j[k]) - 2.0 * dot
                ok = (c_i[rs] == c_j[k]) & (self_id[k][rs] != lane)
                dist.append(jnp.where(ok, t, FAR))
            low = jnp.minimum(jnp.minimum(dist[0], dist[1]), jnp.minimum(dist[2], dist[3]))
            near = jnp.min(low, axis=1, keepdims=True)
            w = [jnp.exp((near - t) * (1.0 / kernel_width)) for t in dist]
            total = jnp.sum((w[0] + w[1]) + (w[2] + w[3]), axis=1, keepdims=True)
            inv = 1.0 / total
            for k in range(K):
                aff[j, rs, k * TILE:(k + 1) * TILE] = (w[k] * inv).astype(jnp.bfloat16)
        return carry

    def spread(j, labels):
        r = 2 * j + a
        acc = None
        for k in range(K):
            part = jnp.dot(aff[j, :, k * TILE:(k + 1) * TILE], labels[tile_of(r, k)],
                           preferred_element_type=jnp.float32)
            acc = part if acc is None else acc + part
        seeds = l0[r].astype(jnp.float32)
        return (spread_weight * acc + (1.0 - spread_weight) * seeds).astype(jnp.bfloat16)

    @pl.when(is_centre)
    def _():
        l0[g] = sd[...]
        for t in range(8):
            cl[t] = jnp.broadcast_to(wide(clu, t).astype(jnp.float32), (8, TILE))
        pltpu.make_async_copy(emb, x0.at[a, pl.ds(0, 8)], lsem.at[0]).wait()

        def chunk(d, q):
            if d > 0:
                arrived(x0.at[0, rows(0)], rx.at[d, q])
                fwd_x(d, q).start()

        def partners(d, q):
            arrived(x0.at[0, rows(0)], fx.at[d, q])
            norms(d, q * PT, q * PT + PT)

        def pass_on(q):
            arrived(relay.at[rows(q)], rrl.at[q])
            from_relay(q).start()

        def gather(steps):
            last = None
            for step in steps:
                chunk(*step)
                if last is not None:
                    partners(*last)
                last = step
            partners(*last)

        gather([(0, q) for q in range(CH)])
        for q in (0, 2):
            pass_on(q)
        gather([(1, 0), (3, 0)])
        for q in (1, 3):
            pass_on(q)
        gather([(d, q) for q in range(1, CH) for d in (1, 3)])

        @pl.when(has_next)
        def _():
            for d in range(4):
                arrived(x0.at[0, pl.ds(8, SPILL)], rsp.at[d])
                fwd_sp(d).start()
            arrived(cs, rcs.at[0])
            for d in range(4):
                arrived(x0.at[0, pl.ds(8, SPILL)], fsp.at[d])

        for t in range(2):
            cl[8 + t] = jnp.broadcast_to(wide(cs, t).astype(jnp.float32), (8, TILE))
        for d in range(4):
            norms(d, 8, 10)
        for d in (0, 1, 3):
            products(d)
        gather([(2, q) for q in (0, 2, 1, 3)])
        products(2)
        for d in (1, 2, 3):
            arrived(l0.at[0], rsd.at[d])
            fwd_seed(d).start()

        @pl.when(has_next)
        def _():
            arrived(l0.at[0], rsd.at[4])
            fwd_seed(4).start()

        def seeds_here():
            for d in range(4):
                arrived(l0.at[0], fsd.at[d])

            @pl.when(has_next)
            def _():
                arrived(l0.at[0], fsd.at[4])

        for j in range(4):
            softmax(j, 0)
            if j == 0:
                seeds_here()
            l1[2 * j + a] = spread(j, l0)
            send_l1(j).start()
            if j == 0:
                @pl.when(has_prev)
                def _():
                    spill_l1().start()

        @pl.when(has_next)
        def _():
            arrived(l1.at[0], rl1s.at[0])
            fwd_l1().start()

        for j in range(4):
            arrived(l1.at[0], rl1.at[j])

        @pl.when(has_next)
        def _():
            arrived(l1.at[0], rl1s.at[1])

        for j in range(4):
            res[j] = spread(j, l1)

            @pl.when(c == j)
            def _(j=j):
                own_result(j).start()

            @pl.when(c != j)
            def _(j=j):
                result(j).start()

        for j in range(4):
            send_l1(j).wait_send()

            @pl.when(c == j)
            def _(j=j):
                own_result(j).wait()

            @pl.when(c != j)
            def _(j=j):
                result(j).wait_send()
        own_l().wait_send()
        for q in range(CH):
            own_x(q).wait_send()
            for d in (1, 2, 3):
                fwd_x(d, q).wait_send()
        for d in (1, 2, 3):
            fwd_seed(d).wait_send()
        for q in range(CH):
            from_relay(q).wait_send()

        @pl.when(has_next)
        def _():
            for d in range(4):
                fwd_sp(d).wait_send()
            fwd_seed(4).wait_send()
            fwd_l1().wait_send()

        @pl.when(has_prev)
        def _():
            spill_l1().wait_send()

    for d in range(4):
        @pl.when(has_prev & (relp == d))
        def _(d=d):
            spill_x(d).wait_send()

    @pl.when(has_prev & (h == 0))
    def _():
        spill_clu().wait_send()
        spill_seed().wait_send()

    for d in (1, 3):
        @pl.when(rel == d)
        def _(d=d):
            for q in range(CH):
                own_chunk(d, q).wait_send()
            own_seed(d).wait_send()

    @pl.when(rel == 2)
    def _():
        for q in range(CH):
            to_relay(q).wait_send()
        own_seed(2).wait_send()

    @pl.when(jnp.logical_not(is_centre))
    def _():
        arrived(out, ro.at[0])


def local(embeddings, clusters, blocks, counts, seed_mask, prior):
    bf16, f32, i32 = jnp.bfloat16, jnp.float32, jnp.int32
    vmem = pl.BlockSpec(memory_space=pltpu.VMEM)
    smem = pl.BlockSpec(memory_space=pltpu.SMEM)
    anyw = pl.BlockSpec(memory_space=pl.ANY)
    hbm = pl.BlockSpec(memory_space=pltpu.HBM)
    V, D = pltpu.VMEM, pltpu.SemaphoreType.DMA
    x = V((2, 10, TILE, 128), bf16)
    return pl.pallas_call(
        kernel,
        out_shape=jax.ShapeDtypeStruct((TILE, TILE), bf16),
        in_specs=[hbm, vmem, smem, smem, vmem, hbm],
        out_specs=anyw,
        scratch_shapes=[
            x, x, x, x,
            V((8, TILE, 128), bf16),
            V((TILE, TILE), bf16),
            V((TILE, TILE), bf16),
            V((8, 128), i32),
            V((10, TILE, TILE), bf16),
            V((10, TILE, TILE), bf16),
            V((4, TILE, K * TILE), f32),
            V((4, TILE, K * TILE), bf16),
            V((10, 8, TILE), f32),
            V((10, 8, TILE), f32),
            V((4, TILE, TILE), bf16),
            D((2,)), D((4, CH)), D((4, CH)), D((4,)), D((4,)), D((5,)), D((5,)), D((1,)), D((CH,)),
            D((4,)), D((2,)), D((1,)),
            D((CH,)), D((1,)), D((2,)), D((1,)), D((CH,)), D((4, CH)), D((4,)), D((5,)), D((4,)), D((2,)), D((4,)),
        ],
        compiler_params=pltpu.CompilerParams(
            collective_id=0, has_side_effects=True, vmem_limit_bytes=40 * 1024 * 1024),
        name="spread",
    )(embeddings.reshape(8, TILE, 128), clusters.reshape(16, 128), blocks.T, counts,
      seed_mask.reshape(2, 128), prior)


def solution(mesh):
    in_specs = (
        P("shard", "grp"),
        P("shard"),
        P("shard", None),
        P("shard"),
        P(("shard", "grp")),
        P(("shard", "grp"), None),
    )
    out_specs = P(("shard", "grp"), None)
    return jax.shard_map(local, mesh=mesh, in_specs=in_specs, out_specs=out_specs, check_vma=False)
```

```python
import jax
import jax.numpy as jnp
from jax import lax
from jax.experimental import pallas as pl
from jax.experimental.pallas import tpu as pltpu
from jax.sharding import PartitionSpec as P

TILE = 256
K = 4
SPILL = 2
STEPS = 2
kernel_width = 0.06
spread_weight = 0.6

MESH = pl.DeviceIdType.MESH
CH = 4
PT = 2
FAR = 3.0e38
RB = 32
NT = (((1,), (1,)), ((), ()))


def kernel(emb, clu, blk, cnt, msk, pri, out,
           x0, x1, x2, x3, relay, pv, sd, cs, l0, l1, gram, aff, nj, cl, res, own_n, nb,
           lsem, rx, fx, rsp, fsp, rsd, fsd, rcs, rrl, rl1, rl1s, ro,
           rn, rns, fn, fns, sn, sfn, sfns,
           sx, ssp, ssd, scs, srl, sfx, sfsp, sfsd, sl1, sl1s, so):
    xs = (x0, x1, x2, x3)
    shards = lax.axis_size("shard")
    s = lax.axis_index("shard")
    g = lax.axis_index("grp")
    a = g % 2
    h = g // 2

    def centre_of(shard):
        return ((shard % 8) // 2 + 2 * (shard % 2)) % 4

    c = centre_of(s)
    rel = (h + 4 - c) % 4
    cp = centre_of((s + shards - 1) % shards)
    xup, xdown = s // 8 * 8 + (s + 2) % 8, s // 8 * 8 + (s + 6) % 8
    relp = (h + 4 - cp) % 4
    centre = {"grp": 2 * c + a}
    partner = {"grp": 2 * h + 1 - a}
    above = {"shard": s - 1, "grp": 2 * cp + a}
    has_prev = s > 0
    has_next = s < shards - 1
    is_centre = rel == 0

    def member(d):
        return {"grp": 2 * ((c + d) % 4) + a}

    def rcopy(src, dst, ssem, rsem, dev):
        return pltpu.make_async_remote_copy(
            src_ref=src, dst_ref=dst, send_sem=ssem, recv_sem=rsem, device_id=dev, device_id_type=MESH)

    def arrived(ref, sem):
        pltpu.make_async_copy(ref, ref, sem).wait()

    pltpu.make_async_copy(pri, pv, lsem.at[1]).start()
    bar = pltpu.get_barrier_semaphore()

    def greet(dev):
        pl.semaphore_signal(bar, inc=1, device_id=dev, device_id_type=MESH)

    @pl.when(is_centre)
    def _():
        for d in (1, 2, 3):
            greet(member(d))
        greet(partner)
        for n in (xup, xdown):
            greet({"shard": n, "grp": 2 * centre_of(n) + a})
            greet({"shard": n, "grp": 2 * ((centre_of(n) + 2) % 4) + a})

        @pl.when(has_next)
        def _():
            for hh in range(4):
                greet({"shard": s + 1, "grp": 2 * hh + a})

    @pl.when(jnp.logical_not(is_centre))
    def _():
        greet(centre)

    own_slice = pltpu.make_async_copy(emb, x0.at[a, pl.ds(0, 8)], lsem.at[0])
    own_slice.start()

    lane = lax.broadcasted_iota(jnp.int32, (1, TILE), 1)
    rowid = lax.broadcasted_iota(jnp.int32, (TILE, 1), 0)
    eye = rowid == lane

    def wide(ref, t):
        return jnp.concatenate([ref[2 * t:2 * t + 1, :], ref[2 * t + 1:2 * t + 2, :]], axis=1)

    own_prior = pltpu.make_async_copy(pri, pv, lsem.at[1])
    own_prior.wait()
    mask_row = wide(msk, 0).astype(jnp.float32)
    pick = jnp.where(eye, mask_row, 0.0).astype(jnp.bfloat16)
    sd[...] = jnp.dot(pick, pv[...], preferred_element_type=jnp.float32).astype(jnp.bfloat16)

    @pl.when(is_centre & jnp.logical_not(has_next))
    def _():
        for x in xs:
            x[:, 8:10] = jnp.zeros((2, SPILL, TILE, 128), jnp.bfloat16)
        l0[8:10] = jnp.zeros((SPILL, TILE, TILE), jnp.bfloat16)
        l1[8:10] = jnp.zeros((SPILL, TILE, TILE), jnp.bfloat16)
        cs[...] = jnp.zeros((8, 128), jnp.int32)
        nb[:, :, 1] = jnp.zeros((4, 2, 8, TILE), jnp.float32)

    base = has_prev.astype(jnp.int32)

    @pl.when(is_centre)
    def _():
        pl.semaphore_wait(bar, 6 + base)

    @pl.when(jnp.logical_not(is_centre))
    def _():
        pl.semaphore_wait(bar, 1 + base + jnp.where(rel == 2, 2, 0))

    def rows(q):
        return pl.ds(q * PT, PT)

    def own_chunk(d, q):
        return rcopy(emb.at[rows(q)], xs[d].at[a, rows(q)], sx.at[q], rx.at[d, q], centre)

    def to_relay(q):
        via = {"shard": xup, "grp": 2 * ((c + 1) % 4) + a} if q < 2 else {"shard": xdown, "grp": 2 * ((c + 3) % 4) + a}
        return rcopy(emb.at[rows(q)], relay.at[rows(q)], sx.at[q], rrl.at[q], via)

    def from_relay(q):
        n = xdown if q < 2 else xup
        return rcopy(relay.at[rows(q)], x2.at[a, rows(q)], srl.at[q], rx.at[2, q],
                     {"shard": n, "grp": 2 * centre_of(n) + a})

    def own_seed(d):
        return rcopy(sd, l0.at[g], ssd.at[0], rsd.at[d], centre)

    def spill_x(d):
        return rcopy(emb.at[pl.ds(0, SPILL)], xs[d].at[a, pl.ds(8, SPILL)], ssp.at[0], rsp.at[d], above)

    def spill_seed():
        return rcopy(sd, l0.at[8 + a], ssd.at[1], rsd.at[4], above)

    def spill_clu():
        return rcopy(clu.at[pl.ds(0, 8)], cs, scs.at[0], rcs.at[0], above)

    for d in (1, 3):
        @pl.when(rel == d)
        def _(d=d):
            for q in range(CH):
                own_chunk(d, q).start()
            own_seed(d).start()

    @pl.when(rel == 2)
    def _():
        for q in (0, 2, 1, 3):
            to_relay(q).start()
        own_seed(2).start()

    def own_x(q):
        return rcopy(emb.at[rows(q)], x0.at[a, rows(q)], sfx.at[0, q], fx.at[0, q], partner)

    def own_l():
        return rcopy(sd, l0.at[g], ssd.at[0], fsd.at[0], partner)

    @pl.when(is_centre)
    def _():
        for q in range(CH):
            own_x(q).start()
        own_l().start()

    for d in range(4):
        @pl.when(has_prev & (relp == d))
        def _(d=d):
            spill_x(d).start()

    @pl.when(has_prev & (h == 0))
    def _():
        spill_clu().start()
        spill_seed().start()

    own_slice.wait()
    ones = jnp.ones((8, 128), jnp.bfloat16)
    for t in range(8):
        v = x0[a, t].astype(jnp.float32)
        sq = v * v
        big = sq.astype(jnp.bfloat16)
        small = (sq - big.astype(jnp.float32)).astype(jnp.bfloat16)
        n = lax.dot_general(ones, big, NT, preferred_element_type=jnp.float32)
        n += lax.dot_general(ones, small, NT, preferred_element_type=jnp.float32)
        own_n[t:t + 1, :] = n[0:1, :]

    def norm_to_centre():
        return rcopy(own_n, nb.at[rel, a, 0], sn.at[0], rn.at[rel], centre)

    def norm_to_partner():
        return rcopy(own_n, nb.at[0, a, 0], sn.at[0], fn.at[0], partner)

    def spill_norm():
        return rcopy(own_n, nb.at[relp, a, 1], sn.at[1], rns.at[relp], above)

    def fwd_norm(d):
        return rcopy(nb.at[d, a, 0], nb.at[d, a, 0], sfn.at[d], fn.at[d], partner)

    def fwd_spill_norm(d):
        return rcopy(nb.at[d, a, 1], nb.at[d, a, 1], sfns.at[d], fns.at[d], partner)

    @pl.when(is_centre)
    def _():
        norm_to_partner().start()

    @pl.when(jnp.logical_not(is_centre))
    def _():
        norm_to_centre().start()

    @pl.when(has_prev)
    def _():
        spill_norm().start()

    def fwd_x(d, q):
        return rcopy(xs[d].at[a, rows(q)], xs[d].at[a, rows(q)], sfx.at[d, q], fx.at[d, q], partner)

    def fwd_sp(d):
        return rcopy(xs[d].at[a, pl.ds(8, SPILL)], xs[d].at[a, pl.ds(8, SPILL)], sfsp.at[d], fsp.at[d], partner)

    def seed_tile(d):
        return 2 * ((c + d) % 4) + a if d < 4 else 8 + a

    def fwd_seed(d):
        t = seed_tile(d)
        return rcopy(l0.at[t], l0.at[t], sfsd.at[d], fsd.at[d], partner)

    def send_l1(j):
        r = 2 * j + a
        return rcopy(l1.at[r], l1.at[r], sl1.at[j], rl1.at[j], partner)

    def spill_l1():
        return rcopy(l1.at[a], l1.at[8 + a], sl1s.at[0], rl1s.at[0], above)

    def fwd_l1():
        return rcopy(l1.at[8 + a], l1.at[8 + a], sl1s.at[1], rl1s.at[1], partner)

    def result(d):
        j = (c + d) % 4
        return rcopy(res.at[j], out, so.at[d], ro.at[0], member(d))

    def own_result():
        return pltpu.make_async_copy(res.at[c], out, lsem.at[1])

    def pair(x, t):
        return jnp.concatenate([x[0, t], x[1, t]], axis=1)

    def tile_of(r, k):
        return jnp.clip(blk[k, r] - 8 * s, 0, 8 + SPILL - 1)

    def products(j, ds, add):
        r = 2 * j + a
        left = [pair(xs[d], r) for d in ds]
        for k in range(K):
            v = gram[j, :, k * TILE:(k + 1) * TILE] if add else None
            for d, rows_x in zip(ds, left):
                p = lax.dot_general(rows_x, pair(xs[d], tile_of(r, k)), NT, preferred_element_type=jnp.float32)
                v = p if v is None else v + p
            gram[j, :, k * TILE:(k + 1) * TILE] = v

    def column(row):
        return jnp.sum(jnp.where(eye, row, 0.0), axis=1, keepdims=True)

    def softmax(j):
        r = 2 * j + a
        n_i = column(nj[r][0:1, :])
        c_i = column(cl[r][0:1, :])
        n_j, c_j, self_id = [], [], []
        for k in range(K):
            t = tile_of(r, k)
            n_j.append(nj[t][0:1, :])
            c_j.append(jnp.where(k < cnt[r], cl[t][0:1, :], -1.0))
            self_id.append(jnp.where(t == r, rowid, -1))
        for b in range(TILE // RB):
            rs = slice(b * RB, (b + 1) * RB)
            dist = []
            for k in range(K):
                dot = gram[j, rs, k * TILE:(k + 1) * TILE]
                t = (n_i[rs] + n_j[k]) - 2.0 * dot
                ok = (c_i[rs] == c_j[k]) & (self_id[k][rs] != lane)
                dist.append(jnp.where(ok, t, FAR))
            low = jnp.minimum(jnp.minimum(dist[0], dist[1]), jnp.minimum(dist[2], dist[3]))
            near = jnp.min(low, axis=1, keepdims=True)
            w = [jnp.exp((near - t) * (1.0 / kernel_width)) for t in dist]
            total = jnp.sum((w[0] + w[1]) + (w[2] + w[3]), axis=1, keepdims=True)
            inv = 1.0 / total
            for k in range(K):
                aff[j, rs, k * TILE:(k + 1) * TILE] = (w[k] * inv).astype(jnp.bfloat16)

    def spread(j, labels):
        r = 2 * j + a
        acc = None
        for k in range(K):
            part = jnp.dot(aff[j, :, k * TILE:(k + 1) * TILE], labels[tile_of(r, k)],
                           preferred_element_type=jnp.float32)
            acc = part if acc is None else acc + part
        seeds = l0[r].astype(jnp.float32)
        return (spread_weight * acc + (1.0 - spread_weight) * seeds).astype(jnp.bfloat16)

    @pl.when(is_centre)
    def _():
        l0[g] = sd[...]
        for t in range(8):
            cl[t] = jnp.broadcast_to(wide(clu, t).astype(jnp.float32), (8, TILE))

        nb[0, a, 0] = own_n[...]
        for q in (0, 2, 1, 3):
            arrived(relay.at[rows(q)], rrl.at[q])
            from_relay(q).start()
        for q in range(CH):
            for d in (1, 3):
                arrived(x0.at[0, rows(0)], rx.at[d, q])
                fwd_x(d, q).start()

        @pl.when(has_next)
        def _():
            for d in range(4):
                arrived(x0.at[0, pl.ds(8, SPILL)], rsp.at[d])
                fwd_sp(d).start()
            arrived(cs, rcs.at[0])

        for q in range(CH):
            for d in (0, 1, 3):
                arrived(x0.at[0, rows(0)], fx.at[d, q])

        @pl.when(has_next)
        def _():
            for d in range(4):
                arrived(x0.at[0, pl.ds(8, SPILL)], fsp.at[d])

        for t in range(2):
            cl[8 + t] = jnp.broadcast_to(wide(cs, t).astype(jnp.float32), (8, TILE))

        def near(j, carry):
            products(j, (0, 1, 3), False)
            return carry

        lax.fori_loop(0, 4, near, 0)
        for q in (0, 2, 1, 3):
            arrived(x0.at[0, rows(0)], rx.at[2, q])
            fwd_x(2, q).start()
        for d in (1, 2, 3):
            arrived(own_n, rn.at[d])
            fwd_norm(d).start()
            arrived(l0.at[0], rsd.at[d])
            fwd_seed(d).start()

        @pl.when(has_next)
        def _():
            for d in range(4):
                arrived(own_n, rns.at[d])
                fwd_spill_norm(d).start()
            arrived(l0.at[0], rsd.at[4])
            fwd_seed(4).start()

        for q in range(CH):
            arrived(x0.at[0, rows(0)], fx.at[2, q])
        for d in range(4):
            arrived(own_n, fn.at[d])
            arrived(l0.at[0], fsd.at[d])

        @pl.when(has_next)
        def _():
            for d in range(4):
                arrived(own_n, fns.at[d])
            arrived(l0.at[0], fsd.at[4])

        for part, tiles in ((0, 8), (1, SPILL)):
            total = nb[0, 0, part]
            for d, b in ((0, 1), (1, 0), (1, 1), (2, 0), (2, 1), (3, 0), (3, 1)):
                total += nb[d, b, part]
            for t in range(tiles):
                nj[8 * part + t] = jnp.broadcast_to(total[t:t + 1, :], (8, TILE))

        def first_step(j, carry):
            products(j, (2,), True)
            softmax(j)
            l1[2 * j + a] = spread(j, l0)
            send_l1(j).start()

            @pl.when((j == 0) & has_prev)
            def _():
                spill_l1().start()

            return carry

        lax.fori_loop(0, 4, first_step, 0)

        @pl.when(has_next)
        def _():
            arrived(l1.at[0], rl1s.at[0])
            fwd_l1().start()

        for j in range(4):
            arrived(l1.at[0], rl1.at[j])

        @pl.when(has_next)
        def _():
            arrived(l1.at[0], rl1s.at[1])

        for d in (2, 1, 3, 0):
            j = (c + d) % 4
            res[j] = spread(j, l1)
            if d == 0:
                own_result().start()
            else:
                result(d).start()

        for j in range(4):
            send_l1(j).wait_send()
        own_result().wait()
        for d in (1, 2, 3):
            result(d).wait_send()
            fwd_norm(d).wait_send()
        norm_to_partner().wait_send()
        own_l().wait_send()
        for q in range(CH):
            own_x(q).wait_send()
            for d in (1, 2, 3):
                fwd_x(d, q).wait_send()
        for d in (1, 2, 3):
            fwd_seed(d).wait_send()
        for q in range(CH):
            from_relay(q).wait_send()

        @pl.when(has_next)
        def _():
            for d in range(4):
                fwd_sp(d).wait_send()
                fwd_spill_norm(d).wait_send()
            fwd_seed(4).wait_send()
            fwd_l1().wait_send()

        @pl.when(has_prev)
        def _():
            spill_l1().wait_send()

    @pl.when(has_prev)
    def _():
        spill_norm().wait_send()

    for d in range(4):
        @pl.when(has_prev & (relp == d))
        def _(d=d):
            spill_x(d).wait_send()

    @pl.when(has_prev & (h == 0))
    def _():
        spill_clu().wait_send()
        spill_seed().wait_send()

    for d in (1, 3):
        @pl.when(rel == d)
        def _(d=d):
            for q in range(CH):
                own_chunk(d, q).wait_send()
            own_seed(d).wait_send()

    @pl.when(rel == 2)
    def _():
        for q in range(CH):
            to_relay(q).wait_send()
        own_seed(2).wait_send()

    @pl.when(jnp.logical_not(is_centre))
    def _():
        norm_to_centre().wait_send()
        arrived(out, ro.at[0])


def local(embeddings, clusters, blocks, counts, seed_mask, prior):
    bf16, f32, i32 = jnp.bfloat16, jnp.float32, jnp.int32
    vmem = pl.BlockSpec(memory_space=pltpu.VMEM)
    smem = pl.BlockSpec(memory_space=pltpu.SMEM)
    anyw = pl.BlockSpec(memory_space=pl.ANY)
    hbm = pl.BlockSpec(memory_space=pltpu.HBM)
    V, D = pltpu.VMEM, pltpu.SemaphoreType.DMA
    x = V((2, 10, TILE, 128), bf16)
    return pl.pallas_call(
        kernel,
        out_shape=jax.ShapeDtypeStruct((TILE, TILE), bf16),
        in_specs=[hbm, vmem, smem, smem, vmem, hbm],
        out_specs=anyw,
        scratch_shapes=[
            x, x, x, x,
            V((8, TILE, 128), bf16),
            V((TILE, TILE), bf16),
            V((TILE, TILE), bf16),
            V((8, 128), i32),
            V((10, TILE, TILE), bf16),
            V((10, TILE, TILE), bf16),
            V((4, TILE, K * TILE), f32),
            V((4, TILE, K * TILE), bf16),
            V((10, 8, TILE), f32),
            V((10, 8, TILE), f32),
            V((4, TILE, TILE), bf16),
            V((8, TILE), f32),
            V((4, 2, 2, 8, TILE), f32),
            D((2,)), D((4, CH)), D((4, CH)), D((4,)), D((4,)), D((5,)), D((5,)), D((1,)), D((CH,)),
            D((4,)), D((2,)), D((1,)),
            D((4,)), D((4,)), D((4,)), D((4,)), D((2,)), D((4,)), D((4,)),
            D((CH,)), D((1,)), D((2,)), D((1,)), D((CH,)), D((4, CH)), D((4,)), D((5,)), D((4,)), D((2,)), D((4,)),
        ],
        compiler_params=pltpu.CompilerParams(
            collective_id=0, has_side_effects=True, vmem_limit_bytes=60 * 1024 * 1024),
        name="spread",
    )(embeddings.reshape(8, TILE, 128), clusters.reshape(16, 128), blocks.T, counts,
      seed_mask.reshape(2, 128), prior)


def solution(mesh):
    in_specs = (
        P("shard", "grp"),
        P("shard"),
        P("shard", None),
        P("shard"),
        P(("shard", "grp")),
        P(("shard", "grp"), None),
    )
    out_specs = P(("shard", "grp"), None)
    return jax.shard_map(local, mesh=mesh, in_specs=in_specs, out_specs=out_specs, check_vma=False)
```

```python
import jax
import jax.numpy as jnp
from jax import lax
from jax.experimental import pallas as pl
from jax.experimental.pallas import tpu as pltpu
from jax.sharding import PartitionSpec as P

TILE = 256
K = 4
SPILL = 2
STEPS = 2
kernel_width = 0.06
spread_weight = 0.6

MESH = pl.DeviceIdType.MESH
CH = 4
PT = 2
FAR = 3.0e38
RB = 32
NT = (((1,), (1,)), ((), ()))


def kernel(emb, clu, blk, cnt, msk, pri, out,
           x0, x1, x2, x3, relay, pv, sd, cs, l0, l1, gram, aff, nj, cl, res, own_n, nb,
           lsem, rx, fx, rsp, fsp, rsd, fsd, rcs, rrl, rl1, rl1s, ro,
           rn, rns, fn, fns, sn, sfn, sfns,
           sx, ssp, ssd, scs, srl, sfx, sfsp, sfsd, sl1, sl1s, so):
    xs = (x0, x1, x2, x3)
    shards = lax.axis_size("shard")
    s = lax.axis_index("shard")
    g = lax.axis_index("grp")
    a = g % 2
    h = g // 2

    def centre_of(shard):
        return ((shard % 8) // 2 + 2 * (shard % 2)) % 4

    c = centre_of(s)
    rel = (h + 4 - c) % 4
    cp = centre_of((s + shards - 1) % shards)
    xup, xdown = s // 8 * 8 + (s + 2) % 8, s // 8 * 8 + (s + 6) % 8
    relp = (h + 4 - cp) % 4
    centre = {"grp": 2 * c + a}
    partner = {"grp": 2 * h + 1 - a}
    above = {"shard": s - 1, "grp": 2 * cp + a}
    has_prev = s > 0
    has_next = s < shards - 1
    is_centre = rel == 0
    even = s % 2 == 0

    def member(d):
        return {"grp": 2 * ((c + d) % 4) + a}

    def rcopy(src, dst, ssem, rsem, dev):
        return pltpu.make_async_remote_copy(
            src_ref=src, dst_ref=dst, send_sem=ssem, recv_sem=rsem, device_id=dev, device_id_type=MESH)

    def arrived(ref, sem):
        pltpu.make_async_copy(ref, ref, sem).wait()

    pltpu.make_async_copy(pri, pv, lsem.at[1]).start()
    bar = pltpu.get_barrier_semaphore()

    def greet(dev):
        pl.semaphore_signal(bar, inc=1, device_id=dev, device_id_type=MESH)

    @pl.when(is_centre)
    def _():
        for d in (1, 2, 3):
            greet(member(d))
        greet(partner)
        for n in (xup, xdown):
            greet({"shard": n, "grp": 2 * centre_of(n) + a})
            greet({"shard": n, "grp": 2 * ((centre_of(n) + 2) % 4) + a})

        @pl.when(has_next)
        def _():
            for hh in range(4):
                greet({"shard": s + 1, "grp": 2 * hh + a})

    @pl.when(jnp.logical_not(is_centre))
    def _():
        greet(centre)

    own_slice = pltpu.make_async_copy(emb, x0.at[a, pl.ds(0, 8)], lsem.at[0])
    own_slice.start()

    lane = lax.broadcasted_iota(jnp.int32, (1, TILE), 1)
    rowid = lax.broadcasted_iota(jnp.int32, (TILE, 1), 0)
    eye = rowid == lane

    def wide(ref, t):
        return jnp.concatenate([ref[2 * t:2 * t + 1, :], ref[2 * t + 1:2 * t + 2, :]], axis=1)

    own_prior = pltpu.make_async_copy(pri, pv, lsem.at[1])
    own_prior.wait()
    mask_row = wide(msk, 0).astype(jnp.float32)
    pick = jnp.where(eye, mask_row, 0.0).astype(jnp.bfloat16)
    sd[...] = jnp.dot(pick, pv[...], preferred_element_type=jnp.float32).astype(jnp.bfloat16)

    @pl.when(is_centre & jnp.logical_not(has_next))
    def _():
        for x in xs:
            x[:, 8:10] = jnp.zeros((2, SPILL, TILE, 128), jnp.bfloat16)
        l0[8:10] = jnp.zeros((SPILL, TILE, TILE), jnp.bfloat16)
        l1[8:10] = jnp.zeros((SPILL, TILE, TILE), jnp.bfloat16)
        cs[...] = jnp.zeros((8, 128), jnp.int32)
        nb[:, :, 1] = jnp.zeros((4, 2, 8, TILE), jnp.float32)

    base = has_prev.astype(jnp.int32)

    @pl.when(is_centre)
    def _():
        pl.semaphore_wait(bar, 6 + base)

    @pl.when(jnp.logical_not(is_centre))
    def _():
        pl.semaphore_wait(bar, 1 + base + jnp.where(rel == 2, 2, 0))

    def rows(q):
        return pl.ds(q * PT, PT)

    def own_chunk(d, q):
        return rcopy(emb.at[rows(q)], xs[d].at[a, rows(q)], sx.at[q], rx.at[d, q], centre)

    def to_relay(q):
        via = {"shard": xup, "grp": 2 * ((c + 1) % 4) + a} if q < 2 else {"shard": xdown, "grp": 2 * ((c + 3) % 4) + a}
        return rcopy(emb.at[rows(q)], relay.at[rows(q)], sx.at[q], rrl.at[q], via)

    def from_relay(q):
        n = xdown if q < 2 else xup
        return rcopy(relay.at[rows(q)], x2.at[a, rows(q)], srl.at[q], rx.at[2, q],
                     {"shard": n, "grp": 2 * centre_of(n) + a})

    def own_seed(d):
        return rcopy(sd, l0.at[g], ssd.at[0], rsd.at[d], centre)

    def spill_x(d):
        return rcopy(emb.at[pl.ds(0, SPILL)], xs[d].at[a, pl.ds(8, SPILL)], ssp.at[0], rsp.at[d], above)

    def spill_seed():
        return rcopy(sd, l0.at[8 + a], ssd.at[1], rsd.at[4], above)

    def spill_clu():
        return rcopy(clu.at[pl.ds(0, 8)], cs, scs.at[0], rcs.at[0], above)

    for d in (1, 3):
        @pl.when(rel == d)
        def _(d=d):
            for q in range(CH):
                own_chunk(d, q).start()

    @pl.when(rel == 2)
    def _():
        for q in (0, 2, 1, 3):
            if q > 0:
                to_relay(q).start()

        @pl.when(even)
        def _():
            to_relay(0).start()

        @pl.when(jnp.logical_not(even))
        def _():
            own_chunk(2, 0).start()

    def own_x(q):
        return rcopy(emb.at[rows(q)], x0.at[a, rows(q)], sfx.at[0, q], fx.at[0, q], partner)

    def own_l():
        return rcopy(sd, l0.at[g], ssd.at[0], fsd.at[0], partner)

    @pl.when(is_centre)
    def _():
        for q in range(CH):
            own_x(q).start()
        own_l().start()

    for d in range(4):
        @pl.when(has_prev & (relp == d))
        def _(d=d):
            spill_x(d).start()

    @pl.when(has_prev & (h == 0))
    def _():
        spill_clu().start()

    own_slice.wait()
    ones = jnp.ones((8, 128), jnp.bfloat16)
    for t in range(8):
        v = x0[a, t].astype(jnp.float32)
        sq = v * v
        big = sq.astype(jnp.bfloat16)
        small = (sq - big.astype(jnp.float32)).astype(jnp.bfloat16)
        n = lax.dot_general(ones, big, NT, preferred_element_type=jnp.float32)
        n += lax.dot_general(ones, small, NT, preferred_element_type=jnp.float32)
        own_n[t:t + 1, :] = n[0:1, :]

    def norm_to_centre():
        return rcopy(own_n, nb.at[rel, a, 0], sn.at[0], rn.at[rel], centre)

    def norm_to_partner():
        return rcopy(own_n, nb.at[0, a, 0], sn.at[0], fn.at[0], partner)

    def spill_norm():
        return rcopy(own_n, nb.at[relp, a, 1], sn.at[1], rns.at[relp], above)

    def fwd_norm(d):
        return rcopy(nb.at[d, a, 0], nb.at[d, a, 0], sfn.at[d], fn.at[d], partner)

    def fwd_spill_norm(d):
        return rcopy(nb.at[d, a, 1], nb.at[d, a, 1], sfns.at[d], fns.at[d], partner)

    @pl.when(is_centre)
    def _():
        norm_to_partner().start()

    @pl.when(jnp.logical_not(is_centre))
    def _():
        norm_to_centre().start()

    @pl.when(has_prev)
    def _():
        spill_norm().start()

    for d in (1, 3):
        @pl.when(rel == d)
        def _(d=d):
            for q in range(CH):
                own_chunk(d, q).wait_send()
            own_seed(d).start()

    @pl.when(rel == 2)
    def _():
        for q in range(CH):
            to_relay(q).wait_send()
        own_seed(2).start()

    @pl.when(has_prev & (h == 0))
    def _():
        spill_seed().start()

    def fwd_x(d, q):
        return rcopy(xs[d].at[a, rows(q)], xs[d].at[a, rows(q)], sfx.at[d, q], fx.at[d, q], partner)

    def fwd_sp(d):
        return rcopy(xs[d].at[a, pl.ds(8, SPILL)], xs[d].at[a, pl.ds(8, SPILL)], sfsp.at[d], fsp.at[d], partner)

    def seed_tile(d):
        return 2 * ((c + d) % 4) + a if d < 4 else 8 + a

    def fwd_seed(d):
        t = seed_tile(d)
        return rcopy(l0.at[t], l0.at[t], sfsd.at[d], fsd.at[d], partner)

    def send_l1(j):
        r = 2 * j + a
        return rcopy(l1.at[r], l1.at[r], sl1.at[j], rl1.at[j], partner)

    def spill_l1():
        return rcopy(l1.at[a], l1.at[8 + a], sl1s.at[0], rl1s.at[0], above)

    def fwd_l1():
        return rcopy(l1.at[8 + a], l1.at[8 + a], sl1s.at[1], rl1s.at[1], partner)

    def result(d):
        j = (c + d) % 4
        return rcopy(res.at[j], out, so.at[d], ro.at[0], member(d))

    def own_result():
        return pltpu.make_async_copy(res.at[c], out, lsem.at[1])

    def pair(x, t):
        return jnp.concatenate([x[0, t], x[1, t]], axis=1)

    def tile_of(r, k):
        return jnp.clip(blk[k, r] - 8 * s, 0, 8 + SPILL - 1)

    def products(j, ds, add):
        r = 2 * j + a
        left = [pair(xs[d], r) for d in ds]
        for k in range(K):
            v = gram[j, :, k * TILE:(k + 1) * TILE] if add else None
            for d, rows_x in zip(ds, left):
                p = lax.dot_general(rows_x, pair(xs[d], tile_of(r, k)), NT, preferred_element_type=jnp.float32)
                v = p if v is None else v + p
            gram[j, :, k * TILE:(k + 1) * TILE] = v

    def column(row):
        return jnp.sum(jnp.where(eye, row, 0.0), axis=1, keepdims=True)

    def softmax(j):
        r = 2 * j + a
        n_i = column(nj[r][0:1, :])
        c_i = column(cl[r][0:1, :])
        n_j, c_j, self_id = [], [], []
        for k in range(K):
            t = tile_of(r, k)
            n_j.append(nj[t][0:1, :])
            c_j.append(jnp.where(k < cnt[r], cl[t][0:1, :], -1.0))
            self_id.append(jnp.where(t == r, rowid, -1))
        for b in range(TILE // RB):
            rs = slice(b * RB, (b + 1) * RB)
            dist = []
            for k in range(K):
                dot = gram[j, rs, k * TILE:(k + 1) * TILE]
                t = (n_i[rs] + n_j[k]) - 2.0 * dot
                ok = (c_i[rs] == c_j[k]) & (self_id[k][rs] != lane)
                dist.append(jnp.where(ok, t, FAR))
            low = jnp.minimum(jnp.minimum(dist[0], dist[1]), jnp.minimum(dist[2], dist[3]))
            near = jnp.min(low, axis=1, keepdims=True)
            w = [jnp.exp((near - t) * (1.0 / kernel_width)) for t in dist]
            total = jnp.sum((w[0] + w[1]) + (w[2] + w[3]), axis=1, keepdims=True)
            inv = 1.0 / total
            for k in range(K):
                aff[j, rs, k * TILE:(k + 1) * TILE] = (w[k] * inv).astype(jnp.bfloat16)

    def spread(j, labels):
        r = 2 * j + a
        acc = None
        for k in range(K):
            part = jnp.dot(aff[j, :, k * TILE:(k + 1) * TILE], labels[tile_of(r, k)],
                           preferred_element_type=jnp.float32)
            acc = part if acc is None else acc + part
        seeds = l0[r].astype(jnp.float32)
        return (spread_weight * acc + (1.0 - spread_weight) * seeds).astype(jnp.bfloat16)

    @pl.when(is_centre)
    def _():
        l0[g] = sd[...]
        for t in range(8):
            cl[t] = jnp.broadcast_to(wide(clu, t).astype(jnp.float32), (8, TILE))

        nb[0, a, 0] = own_n[...]
        @pl.when(even)
        def _():
            arrived(relay.at[rows(0)], rrl.at[0])
            from_relay(0).start()

        for q in (2, 1, 3):
            arrived(relay.at[rows(q)], rrl.at[q])
            from_relay(q).start()
        for q in range(CH):
            for d in (1, 3):
                arrived(x0.at[0, rows(0)], rx.at[d, q])
                fwd_x(d, q).start()

        @pl.when(has_next)
        def _():
            for d in range(4):
                arrived(x0.at[0, pl.ds(8, SPILL)], rsp.at[d])
                fwd_sp(d).start()
            arrived(cs, rcs.at[0])

        for q in range(CH):
            for d in (0, 1, 3):
                arrived(x0.at[0, rows(0)], fx.at[d, q])

        @pl.when(has_next)
        def _():
            for d in range(4):
                arrived(x0.at[0, pl.ds(8, SPILL)], fsp.at[d])

        for t in range(2):
            cl[8 + t] = jnp.broadcast_to(wide(cs, t).astype(jnp.float32), (8, TILE))

        def near(j, carry):
            products(j, (0, 1, 3), False)
            return carry

        lax.fori_loop(0, 4, near, 0)
        for q in (0, 2, 1, 3):
            arrived(x0.at[0, rows(0)], rx.at[2, q])
            fwd_x(2, q).start()
        for d in (1, 2, 3):
            arrived(own_n, rn.at[d])
            fwd_norm(d).start()
            arrived(l0.at[0], rsd.at[d])
            fwd_seed(d).start()

        @pl.when(has_next)
        def _():
            for d in range(4):
                arrived(own_n, rns.at[d])
                fwd_spill_norm(d).start()
            arrived(l0.at[0], rsd.at[4])
            fwd_seed(4).start()

        for q in range(CH):
            arrived(x0.at[0, rows(0)], fx.at[2, q])
        for d in range(4):
            arrived(own_n, fn.at[d])
            arrived(l0.at[0], fsd.at[d])

        @pl.when(has_next)
        def _():
            for d in range(4):
                arrived(own_n, fns.at[d])
            arrived(l0.at[0], fsd.at[4])

        for part, tiles in ((0, 8), (1, SPILL)):
            total = nb[0, 0, part]
            for d, b in ((0, 1), (1, 0), (1, 1), (2, 0), (2, 1), (3, 0), (3, 1)):
                total += nb[d, b, part]
            for t in range(tiles):
                nj[8 * part + t] = jnp.broadcast_to(total[t:t + 1, :], (8, TILE))

        def first_step(j, carry):
            products(j, (2,), True)
            softmax(j)
            l1[2 * j + a] = spread(j, l0)
            send_l1(j).start()

            @pl.when((j == 0) & has_prev)
            def _():
                spill_l1().start()

            return carry

        lax.fori_loop(0, 4, first_step, 0)

        @pl.when(has_next)
        def _():
            arrived(l1.at[0], rl1s.at[0])
            fwd_l1().start()

        for j in range(4):
            arrived(l1.at[0], rl1.at[j])

        @pl.when(has_next)
        def _():
            arrived(l1.at[0], rl1s.at[1])

        for d in (2, 1, 3, 0):
            j = (c + d) % 4
            res[j] = spread(j, l1)
            if d == 0:
                own_result().start()
            else:
                result(d).start()

        for j in range(4):
            send_l1(j).wait_send()
        own_result().wait()
        for d in (1, 2, 3):
            result(d).wait_send()
            fwd_norm(d).wait_send()
        norm_to_partner().wait_send()
        own_l().wait_send()
        for q in range(CH):
            own_x(q).wait_send()
            for d in (1, 2, 3):
                fwd_x(d, q).wait_send()
        for d in (1, 2, 3):
            fwd_seed(d).wait_send()
        for q in range(1, CH):
            from_relay(q).wait_send()

        @pl.when(even)
        def _():
            from_relay(0).wait_send()

        @pl.when(has_next)
        def _():
            for d in range(4):
                fwd_sp(d).wait_send()
                fwd_spill_norm(d).wait_send()
            fwd_seed(4).wait_send()
            fwd_l1().wait_send()

        @pl.when(has_prev)
        def _():
            spill_l1().wait_send()

    @pl.when(has_prev)
    def _():
        spill_norm().wait_send()

    for d in range(4):
        @pl.when(has_prev & (relp == d))
        def _(d=d):
            spill_x(d).wait_send()

    @pl.when(has_prev & (h == 0))
    def _():
        spill_clu().wait_send()
        spill_seed().wait_send()

    for d in (1, 3):
        @pl.when(rel == d)
        def _(d=d):
            own_seed(d).wait_send()

    @pl.when(rel == 2)
    def _():
        own_seed(2).wait_send()

    @pl.when(jnp.logical_not(is_centre))
    def _():
        norm_to_centre().wait_send()
        arrived(out, ro.at[0])


def local(embeddings, clusters, blocks, counts, seed_mask, prior):
    bf16, f32, i32 = jnp.bfloat16, jnp.float32, jnp.int32
    vmem = pl.BlockSpec(memory_space=pltpu.VMEM)
    smem = pl.BlockSpec(memory_space=pltpu.SMEM)
    anyw = pl.BlockSpec(memory_space=pl.ANY)
    hbm = pl.BlockSpec(memory_space=pltpu.HBM)
    V, D = pltpu.VMEM, pltpu.SemaphoreType.DMA
    x = V((2, 10, TILE, 128), bf16)
    return pl.pallas_call(
        kernel,
        out_shape=jax.ShapeDtypeStruct((TILE, TILE), bf16),
        in_specs=[hbm, vmem, smem, smem, vmem, hbm],
        out_specs=anyw,
        scratch_shapes=[
            x, x, x, x,
            V((8, TILE, 128), bf16),
            V((TILE, TILE), bf16),
            V((TILE, TILE), bf16),
            V((8, 128), i32),
            V((10, TILE, TILE), bf16),
            V((10, TILE, TILE), bf16),
            V((4, TILE, K * TILE), f32),
            V((4, TILE, K * TILE), bf16),
            V((10, 8, TILE), f32),
            V((10, 8, TILE), f32),
            V((4, TILE, TILE), bf16),
            V((8, TILE), f32),
            V((4, 2, 2, 8, TILE), f32),
            D((2,)), D((4, CH)), D((4, CH)), D((4,)), D((4,)), D((5,)), D((5,)), D((1,)), D((CH,)),
            D((4,)), D((2,)), D((1,)),
            D((4,)), D((4,)), D((4,)), D((4,)), D((2,)), D((4,)), D((4,)),
            D((CH,)), D((1,)), D((2,)), D((1,)), D((CH,)), D((4, CH)), D((4,)), D((5,)), D((4,)), D((2,)), D((4,)),
        ],
        compiler_params=pltpu.CompilerParams(
            collective_id=0, has_side_effects=True, vmem_limit_bytes=60 * 1024 * 1024),
        name="spread",
    )(embeddings.reshape(8, TILE, 128), clusters.reshape(16, 128), blocks.T, counts,
      seed_mask.reshape(2, 128), prior)


def solution(mesh):
    in_specs = (
        P("shard", "grp"),
        P("shard"),
        P("shard", None),
        P("shard"),
        P(("shard", "grp")),
        P(("shard", "grp"), None),
    )
    out_specs = P(("shard", "grp"), None)
    return jax.shard_map(local, mesh=mesh, in_specs=in_specs, out_specs=out_specs, check_vma=False)
```

```python
import jax
import jax.numpy as jnp
from jax import lax
from jax.experimental import pallas as pl
from jax.experimental.pallas import tpu as pltpu
from jax.sharding import PartitionSpec as P

TILE = 256
K = 4
SPILL = 2
STEPS = 2
kernel_width = 0.06
spread_weight = 0.6

MESH = pl.DeviceIdType.MESH
CH = 4
EARLY = 1
PT = 8 // CH
FIRST = CH // 4
ORDER = [q + p * CH // 2 for q in range(CH // 2) for p in (0, 1)]
FAR = 3.0e38
RB = 32
NT = (((1,), (1,)), ((), ()))


def kernel(emb, clu, blk, cnt, msk, pri, out,
           x0, x1, x2, x3, relay, pv, sd, cs, l0, l1, gram, aff, nj, cl, res, own_n, nb,
           lsem, rx, fx, rsp, fsp, rsd, fsd, rcs, rrl, rl1, rl1s, ro,
           rn, rns, fn, fns, sn, sfn, sfns,
           sx, ssp, ssd, scs, srl, sfx, sfsp, sfsd, sl1, sl1s, so):
    xs = (x0, x1, x2, x3)
    shards = lax.axis_size("shard")
    s = lax.axis_index("shard")
    g = lax.axis_index("grp")
    a = g % 2
    h = g // 2

    def centre_of(shard):
        return ((shard % 8) // 2 + 2 * (shard % 2)) % 4

    c = centre_of(s)
    rel = (h + 4 - c) % 4
    cp = centre_of((s + shards - 1) % shards)
    xup, xdown = s // 8 * 8 + (s + 2) % 8, s // 8 * 8 + (s + 6) % 8
    relp = (h + 4 - cp) % 4
    centre = {"grp": 2 * c + a}
    partner = {"grp": 2 * h + 1 - a}
    above = {"shard": s - 1, "grp": 2 * cp + a}
    has_prev = s > 0
    has_next = s < shards - 1
    is_centre = rel == 0
    even = s % 2 == 0

    def member(d):
        return {"grp": 2 * ((c + d) % 4) + a}

    def rcopy(src, dst, ssem, rsem, dev):
        return pltpu.make_async_remote_copy(
            src_ref=src, dst_ref=dst, send_sem=ssem, recv_sem=rsem, device_id=dev, device_id_type=MESH)

    def arrived(ref, sem):
        pltpu.make_async_copy(ref, ref, sem).wait()

    pltpu.make_async_copy(pri, pv, lsem.at[1]).start()
    bar = pltpu.get_barrier_semaphore()

    def greet(dev):
        pl.semaphore_signal(bar, inc=1, device_id=dev, device_id_type=MESH)

    @pl.when(is_centre)
    def _():
        for d in (1, 2, 3):
            greet(member(d))
        greet(partner)
        for n in (xup, xdown):
            greet({"shard": n, "grp": 2 * centre_of(n) + a})
            greet({"shard": n, "grp": 2 * ((centre_of(n) + 2) % 4) + a})

        @pl.when(has_next)
        def _():
            for hh in range(4):
                greet({"shard": s + 1, "grp": 2 * hh + a})

    @pl.when(jnp.logical_not(is_centre))
    def _():
        greet(centre)

    own_slice = pltpu.make_async_copy(emb, x0.at[a, pl.ds(0, 8)], lsem.at[0])
    own_slice.start()

    lane = lax.broadcasted_iota(jnp.int32, (1, TILE), 1)
    rowid = lax.broadcasted_iota(jnp.int32, (TILE, 1), 0)
    eye = rowid == lane

    def wide(ref, t):
        return jnp.concatenate([ref[2 * t:2 * t + 1, :], ref[2 * t + 1:2 * t + 2, :]], axis=1)

    base = has_prev.astype(jnp.int32)

    @pl.when(is_centre)
    def _():
        pl.semaphore_wait(bar, 6 + base)

    @pl.when(jnp.logical_not(is_centre))
    def _():
        pl.semaphore_wait(bar, 1 + base + jnp.where(rel == 2, 2, 0))

    def rows(q):
        return pl.ds(q * PT, PT)

    def own_chunk(d, q):
        return rcopy(emb.at[rows(q)], xs[d].at[a, rows(q)], sx.at[q], rx.at[d, q], centre)

    def to_relay(q):
        via = {"shard": xup, "grp": 2 * ((c + 1) % 4) + a} if q < CH // 2 else {"shard": xdown, "grp": 2 * ((c + 3) % 4) + a}
        return rcopy(emb.at[rows(q)], relay.at[rows(q)], sx.at[q], rrl.at[q], via)

    def from_relay(q):
        n = xdown if q < CH // 2 else xup
        return rcopy(relay.at[rows(q)], x2.at[a, rows(q)], srl.at[q], rx.at[2, q],
                     {"shard": n, "grp": 2 * centre_of(n) + a})

    def own_seed(d):
        return rcopy(sd, l0.at[g], ssd.at[0], rsd.at[d], centre)

    def spill_x(d):
        return rcopy(emb.at[pl.ds(0, SPILL)], xs[d].at[a, pl.ds(8, SPILL)], ssp.at[0], rsp.at[d], above)

    def spill_seed():
        return rcopy(sd, l0.at[8 + a], ssd.at[1], rsd.at[4], above)

    def spill_clu():
        return rcopy(clu.at[pl.ds(0, 8)], cs, scs.at[0], rcs.at[0], above)

    for d in (1, 3):
        @pl.when(rel == d)
        def _(d=d):
            for q in range(CH):
                own_chunk(d, q).start()

    @pl.when(rel == 2)
    def _():
        for q in ORDER:
            if q >= FIRST:
                to_relay(q).start()

        @pl.when(even)
        def _():
            for q in range(FIRST):
                to_relay(q).start()

        @pl.when(jnp.logical_not(even))
        def _():
            for q in range(FIRST):
                own_chunk(2, q).start()

    def own_x(q):
        return rcopy(emb.at[rows(q)], x0.at[a, rows(q)], sfx.at[0, q], fx.at[0, q], partner)

    def own_l():
        return rcopy(sd, l0.at[g], ssd.at[0], fsd.at[0], partner)

    @pl.when(is_centre)
    def _():
        for q in range(CH):
            own_x(q).start()

    for d in range(4):
        @pl.when(has_prev & (relp == d))
        def _(d=d):
            spill_x(d).start()

    @pl.when(has_prev & (h == 0))
    def _():
        spill_clu().start()

    own_prior = pltpu.make_async_copy(pri, pv, lsem.at[1])
    own_prior.wait()
    mask_row = wide(msk, 0).astype(jnp.float32)
    pick = jnp.where(eye, mask_row, 0.0).astype(jnp.bfloat16)
    sd[...] = jnp.dot(pick, pv[...], preferred_element_type=jnp.float32).astype(jnp.bfloat16)

    @pl.when(is_centre & jnp.logical_not(has_next))
    def _():
        for x in xs:
            x[:, 8:10] = jnp.zeros((2, SPILL, TILE, 128), jnp.bfloat16)
        l0[8:10] = jnp.zeros((SPILL, TILE, TILE), jnp.bfloat16)
        l1[8:10] = jnp.zeros((SPILL, TILE, TILE), jnp.bfloat16)
        cs[...] = jnp.zeros((8, 128), jnp.int32)
        nb[:, :, 1] = jnp.zeros((4, 2, 8, TILE), jnp.float32)

    @pl.when(is_centre)
    def _():
        own_l().start()

    own_slice.wait()
    ones = jnp.ones((8, 128), jnp.bfloat16)
    for t in range(8):
        v = x0[a, t].astype(jnp.float32)
        sq = v * v
        big = sq.astype(jnp.bfloat16)
        small = (sq - big.astype(jnp.float32)).astype(jnp.bfloat16)
        n = lax.dot_general(ones, big, NT, preferred_element_type=jnp.float32)
        n += lax.dot_general(ones, small, NT, preferred_element_type=jnp.float32)
        own_n[t:t + 1, :] = n[0:1, :]

    def norm_to_centre():
        return rcopy(own_n, nb.at[rel, a, 0], sn.at[0], rn.at[rel], centre)

    def norm_to_partner():
        return rcopy(own_n, nb.at[0, a, 0], sn.at[0], fn.at[0], partner)

    def spill_norm():
        return rcopy(own_n, nb.at[relp, a, 1], sn.at[1], rns.at[relp], above)

    def fwd_norm(d):
        return rcopy(nb.at[d, a, 0], nb.at[d, a, 0], sfn.at[d], fn.at[d], partner)

    def fwd_spill_norm(d):
        return rcopy(nb.at[d, a, 1], nb.at[d, a, 1], sfns.at[d], fns.at[d], partner)

    @pl.when(is_centre)
    def _():
        norm_to_partner().start()

    @pl.when(jnp.logical_not(is_centre))
    def _():
        norm_to_centre().start()

    @pl.when(has_prev)
    def _():
        spill_norm().start()

    for d in (1, 3):
        @pl.when(rel == d)
        def _(d=d):
            for q in range(CH):
                own_chunk(d, q).wait_send()
            own_seed(d).start()

    @pl.when(rel == 2)
    def _():
        for q in range(CH):
            to_relay(q).wait_send()
        own_seed(2).start()

    @pl.when(has_prev & (h == 0))
    def _():
        spill_seed().start()

    def fwd_x(d, q):
        return rcopy(xs[d].at[a, rows(q)], xs[d].at[a, rows(q)], sfx.at[d, q], fx.at[d, q], partner)

    def fwd_sp(d):
        return rcopy(xs[d].at[a, pl.ds(8, SPILL)], xs[d].at[a, pl.ds(8, SPILL)], sfsp.at[d], fsp.at[d], partner)

    def seed_tile(d):
        return 2 * ((c + d) % 4) + a if d < 4 else 8 + a

    def fwd_seed(d):
        t = seed_tile(d)
        return rcopy(l0.at[t], l0.at[t], sfsd.at[d], fsd.at[d], partner)

    def send_l1(j):
        r = 2 * j + a
        return rcopy(l1.at[r], l1.at[r], sl1.at[j], rl1.at[j], partner)

    def spill_l1():
        return rcopy(l1.at[a], l1.at[8 + a], sl1s.at[0], rl1s.at[0], above)

    def fwd_l1():
        return rcopy(l1.at[8 + a], l1.at[8 + a], sl1s.at[1], rl1s.at[1], partner)

    def result(d):
        j = (c + d) % 4
        return rcopy(res.at[j], out, so.at[d], ro.at[0], member(d))

    def own_result():
        return pltpu.make_async_copy(res.at[c], out, lsem.at[1])

    def pair(x, t):
        return jnp.concatenate([x[0, t], x[1, t]], axis=1)

    def tile_of(r, k):
        return jnp.clip(blk[k, r] - 8 * s, 0, 8 + SPILL - 1)

    def products(j, ds, add):
        r = 2 * j + a
        left = [pair(xs[d], r) for d in ds]
        for k in range(K):
            v = gram[j, :, k * TILE:(k + 1) * TILE] if add else None
            for d, rows_x in zip(ds, left):
                p = lax.dot_general(rows_x, pair(xs[d], tile_of(r, k)), NT, preferred_element_type=jnp.float32)
                v = p if v is None else v + p
            gram[j, :, k * TILE:(k + 1) * TILE] = v

    def column(row):
        return jnp.sum(jnp.where(eye, row, 0.0), axis=1, keepdims=True)

    def softmax(j):
        r = 2 * j + a
        n_i = column(nj[r][0:1, :])
        c_i = column(cl[r][0:1, :])
        n_j, c_j, self_id = [], [], []
        for k in range(K):
            t = tile_of(r, k)
            n_j.append(nj[t][0:1, :])
            c_j.append(jnp.where(k < cnt[r], cl[t][0:1, :], -1.0))
            self_id.append(jnp.where(t == r, rowid, -1))
        for b in range(TILE // RB):
            rs = slice(b * RB, (b + 1) * RB)
            dist = []
            for k in range(K):
                dot = gram[j, rs, k * TILE:(k + 1) * TILE]
                t = (n_i[rs] + n_j[k]) - 2.0 * dot
                ok = (c_i[rs] == c_j[k]) & (self_id[k][rs] != lane)
                dist.append(jnp.where(ok, t, FAR))
            low = jnp.minimum(jnp.minimum(dist[0], dist[1]), jnp.minimum(dist[2], dist[3]))
            near = jnp.min(low, axis=1, keepdims=True)
            w = [jnp.exp((near - t) * (1.0 / kernel_width)) for t in dist]
            total = jnp.sum((w[0] + w[1]) + (w[2] + w[3]), axis=1, keepdims=True)
            inv = 1.0 / total
            for k in range(K):
                aff[j, rs, k * TILE:(k + 1) * TILE] = (w[k] * inv).astype(jnp.bfloat16)

    def spread(j, labels):
        r = 2 * j + a
        acc = None
        for k in range(K):
            part = jnp.dot(aff[j, :, k * TILE:(k + 1) * TILE], labels[tile_of(r, k)],
                           preferred_element_type=jnp.float32)
            acc = part if acc is None else acc + part
        seeds = l0[r].astype(jnp.float32)
        return (spread_weight * acc + (1.0 - spread_weight) * seeds).astype(jnp.bfloat16)

    @pl.when(is_centre)
    def _():
        l0[g] = sd[...]
        for t in range(8):
            cl[t] = jnp.broadcast_to(wide(clu, t).astype(jnp.float32), (8, TILE))

        nb[0, a, 0] = own_n[...]
        @pl.when(even)
        def _():
            for q in range(FIRST):
                arrived(relay.at[rows(q)], rrl.at[q])
                from_relay(q).start()

        for q in [q for q in ORDER if q >= FIRST]:
            arrived(relay.at[rows(q)], rrl.at[q])
            from_relay(q).start()
        for q in range(CH):
            for d in (1, 3):
                arrived(x0.at[0, rows(0)], rx.at[d, q])
                fwd_x(d, q).start()

        @pl.when(has_next)
        def _():
            for d in range(4):
                arrived(x0.at[0, pl.ds(8, SPILL)], rsp.at[d])
                fwd_sp(d).start()
            arrived(cs, rcs.at[0])

        for q in range(CH):
            for d in (0, 1, 3):
                arrived(x0.at[0, rows(0)], fx.at[d, q])

        @pl.when(has_next)
        def _():
            for d in range(4):
                arrived(x0.at[0, pl.ds(8, SPILL)], fsp.at[d])

        for t in range(2):
            cl[8 + t] = jnp.broadcast_to(wide(cs, t).astype(jnp.float32), (8, TILE))

        def near(j, carry):
            products(j, (0, 1, 3), False)
            return carry

        lax.fori_loop(0, 4, near, 0)
        for q in ORDER:
            arrived(x0.at[0, rows(0)], rx.at[2, q])
            fwd_x(2, q).start()
        for d in (1, 2, 3):
            arrived(own_n, rn.at[d])
            fwd_norm(d).start()

        @pl.when(has_next)
        def _():
            for d in range(4):
                arrived(own_n, rns.at[d])
                fwd_spill_norm(d).start()

        for q in range(CH):
            arrived(x0.at[0, rows(0)], fx.at[2, q])
        for d in range(4):
            arrived(own_n, fn.at[d])

        @pl.when(has_next)
        def _():
            for d in range(4):
                arrived(own_n, fns.at[d])

        for part, tiles in ((0, 8), (1, SPILL)):
            total = nb[0, 0, part]
            for d, b in ((0, 1), (1, 0), (1, 1), (2, 0), (2, 1), (3, 0), (3, 1)):
                total += nb[d, b, part]
            for t in range(tiles):
                nj[8 * part + t] = jnp.broadcast_to(total[t:t + 1, :], (8, TILE))

        def affinity(j, carry):
            products(j, (2,), True)
            softmax(j)
            return carry

        def first_step(j, carry):
            l1[2 * j + a] = spread(j, l0)
            send_l1(j).start()

            @pl.when((j == 0) & has_prev)
            def _():
                spill_l1().start()

            return carry

        lax.fori_loop(0, EARLY, affinity, 0)
        for d in (1, 3, 2):
            arrived(l0.at[0], rsd.at[d])
            fwd_seed(d).start()

        @pl.when(has_next)
        def _():
            arrived(l0.at[0], rsd.at[4])
            fwd_seed(4).start()

        for d in range(4):
            arrived(l0.at[0], fsd.at[d])

        @pl.when(has_next)
        def _():
            arrived(l0.at[0], fsd.at[4])

        lax.fori_loop(0, EARLY, first_step, 0)

        def rest(j, carry):
            affinity(j, 0)
            return first_step(j, carry)

        lax.fori_loop(EARLY, 4, rest, 0)

        @pl.when(has_next)
        def _():
            arrived(l1.at[0], rl1s.at[0])
            fwd_l1().start()

        for j in range(4):
            arrived(l1.at[0], rl1.at[j])

        @pl.when(has_next)
        def _():
            arrived(l1.at[0], rl1s.at[1])

        for d in (1, 2, 3, 0):
            j = (c + d) % 4
            res[j] = spread(j, l1)
            if d == 0:
                own_result().start()
            else:
                result(d).start()

        for j in range(4):
            send_l1(j).wait_send()
        own_result().wait()
        for d in (1, 2, 3):
            result(d).wait_send()
            fwd_norm(d).wait_send()
        norm_to_partner().wait_send()
        own_l().wait_send()
        for q in range(CH):
            own_x(q).wait_send()
            for d in (1, 2, 3):
                fwd_x(d, q).wait_send()
        for d in (1, 2, 3):
            fwd_seed(d).wait_send()
        for q in range(FIRST, CH):
            from_relay(q).wait_send()

        @pl.when(even)
        def _():
            for q in range(FIRST):
                from_relay(q).wait_send()

        @pl.when(has_next)
        def _():
            for d in range(4):
                fwd_sp(d).wait_send()
                fwd_spill_norm(d).wait_send()
            fwd_seed(4).wait_send()
            fwd_l1().wait_send()

        @pl.when(has_prev)
        def _():
            spill_l1().wait_send()

    @pl.when(has_prev)
    def _():
        spill_norm().wait_send()

    for d in range(4):
        @pl.when(has_prev & (relp == d))
        def _(d=d):
            spill_x(d).wait_send()

    @pl.when(has_prev & (h == 0))
    def _():
        spill_clu().wait_send()
        spill_seed().wait_send()

    for d in (1, 3):
        @pl.when(rel == d)
        def _(d=d):
            own_seed(d).wait_send()

    @pl.when(rel == 2)
    def _():
        own_seed(2).wait_send()

    @pl.when(jnp.logical_not(is_centre))
    def _():
        norm_to_centre().wait_send()
        arrived(out, ro.at[0])


def local(embeddings, clusters, blocks, counts, seed_mask, prior):
    bf16, f32, i32 = jnp.bfloat16, jnp.float32, jnp.int32
    vmem = pl.BlockSpec(memory_space=pltpu.VMEM)
    smem = pl.BlockSpec(memory_space=pltpu.SMEM)
    anyw = pl.BlockSpec(memory_space=pl.ANY)
    hbm = pl.BlockSpec(memory_space=pltpu.HBM)
    V, D = pltpu.VMEM, pltpu.SemaphoreType.DMA
    x = V((2, 10, TILE, 128), bf16)
    return pl.pallas_call(
        kernel,
        out_shape=jax.ShapeDtypeStruct((TILE, TILE), bf16),
        in_specs=[hbm, vmem, smem, smem, vmem, hbm],
        out_specs=anyw,
        scratch_shapes=[
            x, x, x, x,
            V((8, TILE, 128), bf16),
            V((TILE, TILE), bf16),
            V((TILE, TILE), bf16),
            V((8, 128), i32),
            V((10, TILE, TILE), bf16),
            V((10, TILE, TILE), bf16),
            V((4, TILE, K * TILE), f32),
            V((4, TILE, K * TILE), bf16),
            V((10, 8, TILE), f32),
            V((10, 8, TILE), f32),
            V((4, TILE, TILE), bf16),
            V((8, TILE), f32),
            V((4, 2, 2, 8, TILE), f32),
            D((2,)), D((4, CH)), D((4, CH)), D((4,)), D((4,)), D((5,)), D((5,)), D((1,)), D((CH,)),
            D((4,)), D((2,)), D((1,)),
            D((4,)), D((4,)), D((4,)), D((4,)), D((2,)), D((4,)), D((4,)),
            D((CH,)), D((1,)), D((2,)), D((1,)), D((CH,)), D((4, CH)), D((4,)), D((5,)), D((4,)), D((2,)), D((4,)),
        ],
        compiler_params=pltpu.CompilerParams(
            collective_id=0, has_side_effects=True, vmem_limit_bytes=60 * 1024 * 1024),
        name="spread",
    )(embeddings.reshape(8, TILE, 128), clusters.reshape(16, 128), blocks.T, counts,
      seed_mask.reshape(2, 128), prior)


def solution(mesh):
    in_specs = (
        P("shard", "grp"),
        P("shard"),
        P("shard", None),
        P("shard"),
        P(("shard", "grp")),
        P(("shard", "grp"), None),
    )
    out_specs = P(("shard", "grp"), None)
    return jax.shard_map(local, mesh=mesh, in_specs=in_specs, out_specs=out_specs, check_vma=False)
```

```python
import jax
import jax.numpy as jnp
from jax import lax
from jax.experimental import pallas as pl
from jax.experimental.pallas import tpu as pltpu
from jax.sharding import PartitionSpec as P

TILE = 256
K = 4
SPILL = 2
STEPS = 2
kernel_width = 0.06
spread_weight = 0.6

MESH = pl.DeviceIdType.MESH
CH = 4
EARLY = 1
PT = 8 // CH
FIRST = CH // 4
ORDER = [q + p * CH // 2 for q in range(CH // 2) for p in (0, 1)]
FAR = 3.0e38
RB = 32
NT = (((1,), (1,)), ((), ()))


def kernel(emb, clu_h, blk_h, cnt_h, msk_h, pri, out,
           x0, x1, x2, x3, relay, pv, sd, cs, l0, l1, gram, aff, nj, cl, res, own_n, nb, clu, blk, cnt, msk,
           lsem, rx, fx, rsp, fsp, rsd, fsd, rcs, rrl, rl1, rl1s, ro,
           rn, rns, fn, fns, sn, sfn, sfns,
           sx, ssp, ssd, scs, srl, sfx, sfsp, sfsd, sl1, sl1s, so):
    xs = (x0, x1, x2, x3)
    shards = lax.axis_size("shard")
    s = lax.axis_index("shard")
    g = lax.axis_index("grp")
    a = g % 2
    h = g // 2

    def centre_of(shard):
        return ((shard % 8) // 2 + 2 * (shard % 2)) % 4

    c = centre_of(s)
    rel = (h + 4 - c) % 4
    cp = centre_of((s + shards - 1) % shards)
    xup, xdown = s // 8 * 8 + (s + 2) % 8, s // 8 * 8 + (s + 6) % 8
    relp = (h + 4 - cp) % 4
    centre = {"grp": 2 * c + a}
    partner = {"grp": 2 * h + 1 - a}
    above = {"shard": s - 1, "grp": 2 * cp + a}
    has_prev = s > 0
    has_next = s < shards - 1
    is_centre = rel == 0
    even = s % 2 == 0

    def member(d):
        return {"grp": 2 * ((c + d) % 4) + a}

    def rcopy(src, dst, ssem, rsem, dev):
        return pltpu.make_async_remote_copy(
            src_ref=src, dst_ref=dst, send_sem=ssem, recv_sem=rsem, device_id=dev, device_id_type=MESH)

    def arrived(ref, sem):
        pltpu.make_async_copy(ref, ref, sem).wait()

    small = [pltpu.make_async_copy(src, dst, lsem.at[2 + i]) for i, (src, dst) in enumerate(
        ((msk_h, msk), (clu_h, clu), (blk_h, blk), (cnt_h, cnt)))]
    for copy in small:
        copy.start()
    pltpu.make_async_copy(pri, pv, lsem.at[1]).start()
    bar = pltpu.get_barrier_semaphore()

    def greet(dev):
        pl.semaphore_signal(bar, inc=1, device_id=dev, device_id_type=MESH)

    @pl.when(is_centre)
    def _():
        for d in (1, 2, 3):
            greet(member(d))
        greet(partner)
        for n in (xup, xdown):
            greet({"shard": n, "grp": 2 * centre_of(n) + a})
            greet({"shard": n, "grp": 2 * ((centre_of(n) + 2) % 4) + a})

        @pl.when(has_next)
        def _():
            for hh in range(4):
                greet({"shard": s + 1, "grp": 2 * hh + a})

    @pl.when(jnp.logical_not(is_centre))
    def _():
        greet(centre)

    own_slice = pltpu.make_async_copy(emb, x0.at[a, pl.ds(0, 8)], lsem.at[0])
    own_slice.start()

    lane = lax.broadcasted_iota(jnp.int32, (1, TILE), 1)
    rowid = lax.broadcasted_iota(jnp.int32, (TILE, 1), 0)
    eye = rowid == lane

    def wide(ref, t):
        return jnp.concatenate([ref[2 * t:2 * t + 1, :], ref[2 * t + 1:2 * t + 2, :]], axis=1)

    base = has_prev.astype(jnp.int32)

    @pl.when(is_centre)
    def _():
        pl.semaphore_wait(bar, 6 + base)

    @pl.when(jnp.logical_not(is_centre))
    def _():
        pl.semaphore_wait(bar, 1 + base + jnp.where(rel == 2, 2, 0))

    def rows(q):
        return pl.ds(q * PT, PT)

    def own_chunk(d, q):
        return rcopy(emb.at[rows(q)], xs[d].at[a, rows(q)], sx.at[q], rx.at[d, q], centre)

    def to_relay(q):
        via = {"shard": xup, "grp": 2 * ((c + 1) % 4) + a} if q < CH // 2 else {"shard": xdown, "grp": 2 * ((c + 3) % 4) + a}
        return rcopy(emb.at[rows(q)], relay.at[rows(q)], sx.at[q], rrl.at[q], via)

    def from_relay(q):
        n = xdown if q < CH // 2 else xup
        return rcopy(relay.at[rows(q)], x2.at[a, rows(q)], srl.at[q], rx.at[2, q],
                     {"shard": n, "grp": 2 * centre_of(n) + a})

    def own_seed(d):
        return rcopy(sd, l0.at[g], ssd.at[0], rsd.at[d], centre)

    def spill_x(d):
        return rcopy(emb.at[pl.ds(0, SPILL)], xs[d].at[a, pl.ds(8, SPILL)], ssp.at[0], rsp.at[d], above)

    def spill_seed():
        return rcopy(sd, l0.at[8 + a], ssd.at[1], rsd.at[4], above)

    def spill_clu():
        return rcopy(clu_h.at[pl.ds(0, 8)], cs, scs.at[0], rcs.at[0], above)

    for d in (1, 3):
        @pl.when(rel == d)
        def _(d=d):
            for q in range(CH):
                own_chunk(d, q).start()

    @pl.when(rel == 2)
    def _():
        for q in ORDER:
            if q >= FIRST:
                to_relay(q).start()

        @pl.when(even)
        def _():
            for q in range(FIRST):
                to_relay(q).start()

        @pl.when(jnp.logical_not(even))
        def _():
            for q in range(FIRST):
                own_chunk(2, q).start()

    def own_x(q):
        return rcopy(emb.at[rows(q)], x0.at[a, rows(q)], sfx.at[0, q], fx.at[0, q], partner)

    def own_l():
        return rcopy(sd, l0.at[g], ssd.at[0], fsd.at[0], partner)

    @pl.when(is_centre)
    def _():
        for q in range(CH):
            own_x(q).start()

    for d in range(4):
        @pl.when(has_prev & (relp == d))
        def _(d=d):
            spill_x(d).start()

    @pl.when(has_prev & (h == 0))
    def _():
        spill_clu().start()

    own_prior = pltpu.make_async_copy(pri, pv, lsem.at[1])
    for copy in small:
        copy.wait()
    own_prior.wait()
    mask_row = wide(msk, 0).astype(jnp.float32)
    pick = jnp.where(eye, mask_row, 0.0).astype(jnp.bfloat16)
    sd[...] = jnp.dot(pick, pv[...], preferred_element_type=jnp.float32).astype(jnp.bfloat16)

    @pl.when(is_centre & jnp.logical_not(has_next))
    def _():
        for x in xs:
            x[:, 8:10] = jnp.zeros((2, SPILL, TILE, 128), jnp.bfloat16)
        l0[8:10] = jnp.zeros((SPILL, TILE, TILE), jnp.bfloat16)
        l1[8:10] = jnp.zeros((SPILL, TILE, TILE), jnp.bfloat16)
        cs[...] = jnp.zeros((8, 128), jnp.int32)
        nb[:, :, 1] = jnp.zeros((4, 2, 8, TILE), jnp.float32)

    @pl.when(is_centre)
    def _():
        own_l().start()

    own_slice.wait()
    ones = jnp.ones((8, 128), jnp.bfloat16)
    for t in range(8):
        v = x0[a, t].astype(jnp.float32)
        sq = v * v
        big = sq.astype(jnp.bfloat16)
        small = (sq - big.astype(jnp.float32)).astype(jnp.bfloat16)
        n = lax.dot_general(ones, big, NT, preferred_element_type=jnp.float32)
        n += lax.dot_general(ones, small, NT, preferred_element_type=jnp.float32)
        own_n[t:t + 1, :] = n[0:1, :]

    def norm_to_centre():
        return rcopy(own_n, nb.at[rel, a, 0], sn.at[0], rn.at[rel], centre)

    def norm_to_partner():
        return rcopy(own_n, nb.at[0, a, 0], sn.at[0], fn.at[0], partner)

    def spill_norm():
        return rcopy(own_n, nb.at[relp, a, 1], sn.at[1], rns.at[relp], above)

    def fwd_norm(d):
        return rcopy(nb.at[d, a, 0], nb.at[d, a, 0], sfn.at[d], fn.at[d], partner)

    def fwd_spill_norm(d):
        return rcopy(nb.at[d, a, 1], nb.at[d, a, 1], sfns.at[d], fns.at[d], partner)

    @pl.when(is_centre)
    def _():
        norm_to_partner().start()

    @pl.when(jnp.logical_not(is_centre))
    def _():
        norm_to_centre().start()

    @pl.when(has_prev)
    def _():
        spill_norm().start()

    for d in (1, 3):
        @pl.when(rel == d)
        def _(d=d):
            for q in range(CH):
                own_chunk(d, q).wait_send()
            own_seed(d).start()

    @pl.when(rel == 2)
    def _():
        for q in range(CH):
            to_relay(q).wait_send()
        own_seed(2).start()

    @pl.when(has_prev & (h == 0))
    def _():
        spill_seed().start()

    def fwd_x(d, q):
        return rcopy(xs[d].at[a, rows(q)], xs[d].at[a, rows(q)], sfx.at[d, q], fx.at[d, q], partner)

    def fwd_sp(d):
        return rcopy(xs[d].at[a, pl.ds(8, SPILL)], xs[d].at[a, pl.ds(8, SPILL)], sfsp.at[d], fsp.at[d], partner)

    def seed_tile(d):
        return 2 * ((c + d) % 4) + a if d < 4 else 8 + a

    def fwd_seed(d):
        t = seed_tile(d)
        return rcopy(l0.at[t], l0.at[t], sfsd.at[d], fsd.at[d], partner)

    def send_l1(j):
        r = 2 * j + a
        return rcopy(l1.at[r], l1.at[r], sl1.at[j], rl1.at[j], partner)

    def spill_l1():
        return rcopy(l1.at[a], l1.at[8 + a], sl1s.at[0], rl1s.at[0], above)

    def fwd_l1():
        return rcopy(l1.at[8 + a], l1.at[8 + a], sl1s.at[1], rl1s.at[1], partner)

    def result(d):
        j = (c + d) % 4
        return rcopy(res.at[j], out, so.at[d], ro.at[0], member(d))

    def own_result():
        return pltpu.make_async_copy(res.at[c], out, lsem.at[1])

    def pair(x, t):
        return jnp.concatenate([x[0, t], x[1, t]], axis=1)

    def tile_of(r, k):
        return jnp.clip(blk[k, r] - 8 * s, 0, 8 + SPILL - 1)

    def products(j, ds, add):
        r = 2 * j + a
        left = [pair(xs[d], r) for d in ds]
        for k in range(K):
            v = gram[j, :, k * TILE:(k + 1) * TILE] if add else None
            for d, rows_x in zip(ds, left):
                p = lax.dot_general(rows_x, pair(xs[d], tile_of(r, k)), NT, preferred_element_type=jnp.float32)
                v = p if v is None else v + p
            gram[j, :, k * TILE:(k + 1) * TILE] = v

    def column(row):
        return jnp.sum(jnp.where(eye, row, 0.0), axis=1, keepdims=True)

    def softmax(j):
        r = 2 * j + a
        n_i = column(nj[r][0:1, :])
        c_i = column(cl[r][0:1, :])
        n_j, c_j, self_id = [], [], []
        for k in range(K):
            t = tile_of(r, k)
            n_j.append(nj[t][0:1, :])
            c_j.append(jnp.where(k < cnt[r], cl[t][0:1, :], -1.0))
            self_id.append(jnp.where(t == r, rowid, -1))
        for b in range(TILE // RB):
            rs = slice(b * RB, (b + 1) * RB)
            dist = []
            for k in range(K):
                dot = gram[j, rs, k * TILE:(k + 1) * TILE]
                t = (n_i[rs] + n_j[k]) - 2.0 * dot
                ok = (c_i[rs] == c_j[k]) & (self_id[k][rs] != lane)
                dist.append(jnp.where(ok, t, FAR))
            low = jnp.minimum(jnp.minimum(dist[0], dist[1]), jnp.minimum(dist[2], dist[3]))
            near = jnp.min(low, axis=1, keepdims=True)
            w = [jnp.exp((near - t) * (1.0 / kernel_width)) for t in dist]
            total = jnp.sum((w[0] + w[1]) + (w[2] + w[3]), axis=1, keepdims=True)
            inv = 1.0 / total
            for k in range(K):
                aff[j, rs, k * TILE:(k + 1) * TILE] = (w[k] * inv).astype(jnp.bfloat16)

    def spread(j, labels):
        r = 2 * j + a
        acc = None
        for k in range(K):
            part = jnp.dot(aff[j, :, k * TILE:(k + 1) * TILE], labels[tile_of(r, k)],
                           preferred_element_type=jnp.float32)
            acc = part if acc is None else acc + part
        seeds = l0[r].astype(jnp.float32)
        return (spread_weight * acc + (1.0 - spread_weight) * seeds).astype(jnp.bfloat16)

    @pl.when(is_centre)
    def _():
        l0[g] = sd[...]
        for t in range(8):
            cl[t] = jnp.broadcast_to(wide(clu, t).astype(jnp.float32), (8, TILE))

        nb[0, a, 0] = own_n[...]
        @pl.when(even)
        def _():
            for q in range(FIRST):
                arrived(relay.at[rows(q)], rrl.at[q])
                from_relay(q).start()

        for q in [q for q in ORDER if q >= FIRST]:
            arrived(relay.at[rows(q)], rrl.at[q])
            from_relay(q).start()
        for q in range(CH):
            for d in (1, 3):
                arrived(x0.at[0, rows(0)], rx.at[d, q])
                fwd_x(d, q).start()

        @pl.when(has_next)
        def _():
            for d in range(4):
                arrived(x0.at[0, pl.ds(8, SPILL)], rsp.at[d])
                fwd_sp(d).start()
            arrived(cs, rcs.at[0])

        for q in range(CH):
            for d in (0, 1, 3):
                arrived(x0.at[0, rows(0)], fx.at[d, q])

        @pl.when(has_next)
        def _():
            for d in range(4):
                arrived(x0.at[0, pl.ds(8, SPILL)], fsp.at[d])

        for t in range(2):
            cl[8 + t] = jnp.broadcast_to(wide(cs, t).astype(jnp.float32), (8, TILE))

        def near(j, carry):
            products(j, (0, 1, 3), False)
            return carry

        lax.fori_loop(0, 4, near, 0)
        for q in ORDER:
            arrived(x0.at[0, rows(0)], rx.at[2, q])
            fwd_x(2, q).start()
        for d in (1, 2, 3):
            arrived(own_n, rn.at[d])
            fwd_norm(d).start()

        @pl.when(has_next)
        def _():
            for d in range(4):
                arrived(own_n, rns.at[d])
                fwd_spill_norm(d).start()

        for q in range(CH):
            arrived(x0.at[0, rows(0)], fx.at[2, q])
        for d in range(4):
            arrived(own_n, fn.at[d])

        @pl.when(has_next)
        def _():
            for d in range(4):
                arrived(own_n, fns.at[d])

        for part, tiles in ((0, 8), (1, SPILL)):
            total = nb[0, 0, part]
            for d, b in ((0, 1), (1, 0), (1, 1), (2, 0), (2, 1), (3, 0), (3, 1)):
                total += nb[d, b, part]
            for t in range(tiles):
                nj[8 * part + t] = jnp.broadcast_to(total[t:t + 1, :], (8, TILE))

        def affinity(j, carry):
            products(j, (2,), True)
            softmax(j)
            return carry

        def first_step(j, carry):
            l1[2 * j + a] = spread(j, l0)
            send_l1(j).start()

            @pl.when((j == 0) & has_prev)
            def _():
                spill_l1().start()

            return carry

        lax.fori_loop(0, EARLY, affinity, 0)
        for d in (1, 3, 2):
            arrived(l0.at[0], rsd.at[d])
            fwd_seed(d).start()

        @pl.when(has_next)
        def _():
            arrived(l0.at[0], rsd.at[4])
            fwd_seed(4).start()

        for d in range(4):
            arrived(l0.at[0], fsd.at[d])

        @pl.when(has_next)
        def _():
            arrived(l0.at[0], fsd.at[4])

        lax.fori_loop(0, EARLY, first_step, 0)

        def rest(j, carry):
            affinity(j, 0)
            return first_step(j, carry)

        lax.fori_loop(EARLY, 4, rest, 0)

        @pl.when(has_next)
        def _():
            arrived(l1.at[0], rl1s.at[0])
            fwd_l1().start()

        for j in range(4):
            arrived(l1.at[0], rl1.at[j])

        @pl.when(has_next)
        def _():
            arrived(l1.at[0], rl1s.at[1])

        for d in (1, 2, 3, 0):
            j = (c + d) % 4
            res[j] = spread(j, l1)
            if d == 0:
                own_result().start()
            else:
                result(d).start()

        for j in range(4):
            send_l1(j).wait_send()
        own_result().wait()
        for d in (1, 2, 3):
            result(d).wait_send()
            fwd_norm(d).wait_send()
        norm_to_partner().wait_send()
        own_l().wait_send()
        for q in range(CH):
            own_x(q).wait_send()
            for d in (1, 2, 3):
                fwd_x(d, q).wait_send()
        for d in (1, 2, 3):
            fwd_seed(d).wait_send()
        for q in range(FIRST, CH):
            from_relay(q).wait_send()

        @pl.when(even)
        def _():
            for q in range(FIRST):
                from_relay(q).wait_send()

        @pl.when(has_next)
        def _():
            for d in range(4):
                fwd_sp(d).wait_send()
                fwd_spill_norm(d).wait_send()
            fwd_seed(4).wait_send()
            fwd_l1().wait_send()

        @pl.when(has_prev)
        def _():
            spill_l1().wait_send()

    @pl.when(has_prev)
    def _():
        spill_norm().wait_send()

    for d in range(4):
        @pl.when(has_prev & (relp == d))
        def _(d=d):
            spill_x(d).wait_send()

    @pl.when(has_prev & (h == 0))
    def _():
        spill_clu().wait_send()
        spill_seed().wait_send()

    for d in (1, 3):
        @pl.when(rel == d)
        def _(d=d):
            own_seed(d).wait_send()

    @pl.when(rel == 2)
    def _():
        own_seed(2).wait_send()

    @pl.when(jnp.logical_not(is_centre))
    def _():
        norm_to_centre().wait_send()
        arrived(out, ro.at[0])


def local(embeddings, clusters, blocks, counts, seed_mask, prior):
    bf16, f32, i32 = jnp.bfloat16, jnp.float32, jnp.int32
    anyw = pl.BlockSpec(memory_space=pl.ANY)
    hbm = pl.BlockSpec(memory_space=pltpu.HBM)
    V, D = pltpu.VMEM, pltpu.SemaphoreType.DMA
    x = V((2, 10, TILE, 128), bf16)
    return pl.pallas_call(
        kernel,
        out_shape=jax.ShapeDtypeStruct((TILE, TILE), bf16),
        in_specs=[hbm] * 6,
        out_specs=anyw,
        scratch_shapes=[
            x, x, x, x,
            V((8, TILE, 128), bf16),
            V((TILE, TILE), bf16),
            V((TILE, TILE), bf16),
            V((8, 128), i32),
            V((10, TILE, TILE), bf16),
            V((10, TILE, TILE), bf16),
            V((4, TILE, K * TILE), f32),
            V((4, TILE, K * TILE), bf16),
            V((10, 8, TILE), f32),
            V((10, 8, TILE), f32),
            V((4, TILE, TILE), bf16),
            V((8, TILE), f32),
            V((4, 2, 2, 8, TILE), f32),
            V((16, 128), i32), pltpu.SMEM((4, 8), i32), pltpu.SMEM((8,), i32), V((2, 128), i32),
            D((6,)), D((4, CH)), D((4, CH)), D((4,)), D((4,)), D((5,)), D((5,)), D((1,)), D((CH,)),
            D((4,)), D((2,)), D((1,)),
            D((4,)), D((4,)), D((4,)), D((4,)), D((2,)), D((4,)), D((4,)),
            D((CH,)), D((1,)), D((2,)), D((1,)), D((CH,)), D((4, CH)), D((4,)), D((5,)), D((4,)), D((2,)), D((4,)),
        ],
        compiler_params=pltpu.CompilerParams(
            collective_id=0, has_side_effects=True, vmem_limit_bytes=60 * 1024 * 1024),
        name="spread",
    )(embeddings.reshape(8, TILE, 128), clusters.reshape(16, 128), blocks.T, counts,
      seed_mask.reshape(2, 128), prior)


def solution(mesh):
    in_specs = (
        P("shard", "grp"),
        P("shard"),
        P("shard", None),
        P("shard"),
        P(("shard", "grp")),
        P(("shard", "grp"), None),
    )
    out_specs = P(("shard", "grp"), None)
    return jax.shard_map(local, mesh=mesh, in_specs=in_specs, out_specs=out_specs, check_vma=False)
```

```python
import jax
import jax.numpy as jnp
from jax import lax
from jax.experimental import pallas as pl
from jax.experimental.pallas import tpu as pltpu
from jax.sharding import PartitionSpec as P

TILE = 256
K = 4
SPILL = 2
STEPS = 2
kernel_width = 0.06
spread_weight = 0.6

MESH = pl.DeviceIdType.MESH
CH = 4
EARLY = 1
PT = 8 // CH
FIRST = CH // 4
ORDER = [q + p * CH // 2 for q in range(CH // 2) for p in (0, 1)]
FAR = 3.0e38
RB = 32
NT = (((1,), (1,)), ((), ()))


def kernel(emb, clu_h, blk_h, cnt_h, msk_h, pri, out,
           x0, x1, x2, x3, relay, pv, sd, cs, l0, l1, gram, aff, nj, cl, res, own_n, nb, clu, blk, cnt, msk,
           lsem, rx, fx, rsp, fsp, rsd, fsd, rcs, rrl, rl1, rl1s, ro,
           rn, rns, fn, fns, sn, sfn, sfns,
           sx, ssp, ssd, scs, srl, sfx, sfsp, sfsd, sl1, sl1s, so):
    xs = (x0, x1, x2, x3)
    shards = lax.axis_size("shard")
    s = lax.axis_index("shard")
    g = lax.axis_index("grp")
    a = g % 2
    h = g // 2

    def centre_of(shard):
        return ((shard % 8) // 2 + 2 * (shard % 2)) % 4

    c = centre_of(s)
    rel = (h + 4 - c) % 4
    cp = centre_of((s + shards - 1) % shards)
    xup, xdown = s // 8 * 8 + (s + 2) % 8, s // 8 * 8 + (s + 6) % 8
    relp = (h + 4 - cp) % 4
    centre = {"grp": 2 * c + a}
    partner = {"grp": 2 * h + 1 - a}
    above = {"shard": s - 1, "grp": 2 * cp + a}
    has_prev = s > 0
    has_next = s < shards - 1
    is_centre = rel == 0
    even = s % 2 == 0

    def member(d):
        return {"grp": 2 * ((c + d) % 4) + a}

    def rcopy(src, dst, ssem, rsem, dev):
        return pltpu.make_async_remote_copy(
            src_ref=src, dst_ref=dst, send_sem=ssem, recv_sem=rsem, device_id=dev, device_id_type=MESH)

    def arrived(ref, sem):
        pltpu.make_async_copy(ref, ref, sem).wait()

    small = [pltpu.make_async_copy(src, dst, lsem.at[2 + i]) for i, (src, dst) in enumerate(
        ((msk_h, msk), (clu_h, clu), (blk_h, blk), (cnt_h, cnt)))]
    for copy in small:
        copy.start()
    pltpu.make_async_copy(pri, pv, lsem.at[1]).start()
    bar = pltpu.get_barrier_semaphore()

    def greet(dev):
        pl.semaphore_signal(bar, inc=1, device_id=dev, device_id_type=MESH)

    @pl.when(is_centre)
    def _():
        for d in (1, 2, 3):
            greet(member(d))
        greet(partner)
        for n in (xup, xdown):
            greet({"shard": n, "grp": 2 * centre_of(n) + a})
            greet({"shard": n, "grp": 2 * ((centre_of(n) + 2) % 4) + a})

        @pl.when(has_next)
        def _():
            for hh in range(4):
                greet({"shard": s + 1, "grp": 2 * hh + a})

    @pl.when(jnp.logical_not(is_centre))
    def _():
        greet(centre)

    own_slice = pltpu.make_async_copy(emb, x0.at[a, pl.ds(0, 8)], lsem.at[0])
    own_slice.start()

    lane = lax.broadcasted_iota(jnp.int32, (1, TILE), 1)
    rowid = lax.broadcasted_iota(jnp.int32, (TILE, 1), 0)
    eye = rowid == lane

    def wide(ref, t):
        return jnp.concatenate([ref[2 * t:2 * t + 1, :], ref[2 * t + 1:2 * t + 2, :]], axis=1)

    base = has_prev.astype(jnp.int32)

    @pl.when(is_centre)
    def _():
        pl.semaphore_wait(bar, 6 + base)

    @pl.when(jnp.logical_not(is_centre))
    def _():
        pl.semaphore_wait(bar, 1 + base + jnp.where(rel == 2, 2, 0))

    def rows(q):
        return pl.ds(q * PT, PT)

    def own_chunk(d, q):
        return rcopy(emb.at[rows(q)], xs[d].at[a, rows(q)], sx.at[q], rx.at[d, q], centre)

    def to_relay(q):
        via = {"shard": xup, "grp": 2 * ((c + 1) % 4) + a} if q < CH // 2 else {"shard": xdown, "grp": 2 * ((c + 3) % 4) + a}
        return rcopy(emb.at[rows(q)], relay.at[rows(q)], sx.at[q], rrl.at[q], via)

    def from_relay(q):
        n = xdown if q < CH // 2 else xup
        return rcopy(relay.at[rows(q)], x2.at[a, rows(q)], srl.at[q], rx.at[2, q],
                     {"shard": n, "grp": 2 * centre_of(n) + a})

    def own_seed(d):
        return rcopy(sd, l0.at[g], ssd.at[0], rsd.at[d], centre)

    def spill_x(d):
        return rcopy(emb.at[pl.ds(0, SPILL)], xs[d].at[a, pl.ds(8, SPILL)], ssp.at[0], rsp.at[d], above)

    def spill_seed():
        return rcopy(sd, l0.at[8 + a], ssd.at[1], rsd.at[4], above)

    def spill_clu():
        return rcopy(clu_h.at[pl.ds(0, 8)], cs, scs.at[0], rcs.at[0], above)

    for d in (1, 3):
        @pl.when(rel == d)
        def _(d=d):
            for q in range(CH):
                own_chunk(d, q).start()

    @pl.when(rel == 2)
    def _():
        for q in ORDER:
            if q >= FIRST:
                to_relay(q).start()

        @pl.when(even)
        def _():
            for q in range(FIRST):
                to_relay(q).start()

        @pl.when(jnp.logical_not(even))
        def _():
            for q in range(FIRST):
                own_chunk(2, q).start()

    def own_x(q):
        return rcopy(emb.at[rows(q)], x0.at[a, rows(q)], sfx.at[0, q], fx.at[0, q], partner)

    def own_l():
        return rcopy(sd, l0.at[g], ssd.at[0], fsd.at[0], partner)

    @pl.when(is_centre)
    def _():
        for q in range(CH):
            own_x(q).start()

    for d in range(4):
        @pl.when(has_prev & (relp == d))
        def _(d=d):
            spill_x(d).start()

    @pl.when(has_prev & (h == 0))
    def _():
        spill_clu().start()

    own_prior = pltpu.make_async_copy(pri, pv, lsem.at[1])
    for copy in small:
        copy.wait()
    own_prior.wait()
    mask_row = wide(msk, 0).astype(jnp.float32)
    pick = jnp.where(eye, mask_row, 0.0).astype(jnp.bfloat16)
    sd[...] = jnp.dot(pick, pv[...], preferred_element_type=jnp.float32).astype(jnp.bfloat16)

    @pl.when(is_centre & jnp.logical_not(has_next))
    def _():
        for x in xs:
            x[:, 8:10] = jnp.zeros((2, SPILL, TILE, 128), jnp.bfloat16)
        l0[8:10] = jnp.zeros((SPILL, TILE, TILE), jnp.bfloat16)
        l1[8:10] = jnp.zeros((SPILL, TILE, TILE), jnp.bfloat16)
        cs[...] = jnp.zeros((8, 128), jnp.int32)
        nb[:, :, 1] = jnp.zeros((4, 2, 8, TILE), jnp.float32)

    @pl.when(is_centre)
    def _():
        own_l().start()

    own_slice.wait()
    ones = jnp.ones((8, 128), jnp.bfloat16)
    for t in range(8):
        v = x0[a, t].astype(jnp.float32)
        sq = v * v
        big = sq.astype(jnp.bfloat16)
        small = (sq - big.astype(jnp.float32)).astype(jnp.bfloat16)
        n = lax.dot_general(ones, big, NT, preferred_element_type=jnp.float32)
        n += lax.dot_general(ones, small, NT, preferred_element_type=jnp.float32)
        own_n[t:t + 1, :] = n[0:1, :]

    def norm_to_centre():
        return rcopy(own_n, nb.at[rel, a, 0], sn.at[0], rn.at[rel], centre)

    def norm_to_partner():
        return rcopy(own_n, nb.at[0, a, 0], sn.at[0], fn.at[0], partner)

    def spill_norm():
        return rcopy(own_n, nb.at[relp, a, 1], sn.at[1], rns.at[relp], above)

    def fwd_norm(d):
        return rcopy(nb.at[d, a, 0], nb.at[d, a, 0], sfn.at[d], fn.at[d], partner)

    def fwd_spill_norm(d):
        return rcopy(nb.at[d, a, 1], nb.at[d, a, 1], sfns.at[d], fns.at[d], partner)

    @pl.when(is_centre)
    def _():
        norm_to_partner().start()

    @pl.when(jnp.logical_not(is_centre))
    def _():
        norm_to_centre().start()

    @pl.when(has_prev)
    def _():
        spill_norm().start()

    for d in (1, 3):
        @pl.when(rel == d)
        def _(d=d):
            for q in range(CH - 1):
                own_chunk(d, q).wait_send()
            own_seed(d).start()
            own_chunk(d, CH - 1).wait_send()

    @pl.when(rel == 2)
    def _():
        for q in range(CH):
            to_relay(q).wait_send()
        own_seed(2).start()

    @pl.when(has_prev & (h == 0))
    def _():
        spill_seed().start()

    def fwd_x(d, q):
        return rcopy(xs[d].at[a, rows(q)], xs[d].at[a, rows(q)], sfx.at[d, q], fx.at[d, q], partner)

    def fwd_sp(d):
        return rcopy(xs[d].at[a, pl.ds(8, SPILL)], xs[d].at[a, pl.ds(8, SPILL)], sfsp.at[d], fsp.at[d], partner)

    def seed_tile(d):
        return 2 * ((c + d) % 4) + a if d < 4 else 8 + a

    def fwd_seed(d):
        t = seed_tile(d)
        return rcopy(l0.at[t], l0.at[t], sfsd.at[d], fsd.at[d], partner)

    def send_l1(j):
        r = 2 * j + a
        return rcopy(l1.at[r], l1.at[r], sl1.at[j], rl1.at[j], partner)

    def spill_l1():
        return rcopy(l1.at[a], l1.at[8 + a], sl1s.at[0], rl1s.at[0], above)

    def fwd_l1():
        return rcopy(l1.at[8 + a], l1.at[8 + a], sl1s.at[1], rl1s.at[1], partner)

    def result(d):
        j = (c + d) % 4
        return rcopy(res.at[j], out, so.at[d], ro.at[0], member(d))

    def own_result():
        return pltpu.make_async_copy(res.at[c], out, lsem.at[1])

    def pair(x, t):
        return jnp.concatenate([x[0, t], x[1, t]], axis=1)

    def tile_of(r, k):
        return jnp.clip(blk[k, r] - 8 * s, 0, 8 + SPILL - 1)

    def products(j, ds, add):
        r = 2 * j + a
        left = [pair(xs[d], r) for d in ds]
        for k in range(K):
            v = gram[j, :, k * TILE:(k + 1) * TILE] if add else None
            for d, rows_x in zip(ds, left):
                p = lax.dot_general(rows_x, pair(xs[d], tile_of(r, k)), NT, preferred_element_type=jnp.float32)
                v = p if v is None else v + p
            gram[j, :, k * TILE:(k + 1) * TILE] = v

    def column(row):
        return jnp.sum(jnp.where(eye, row, 0.0), axis=1, keepdims=True)

    def softmax(j):
        r = 2 * j + a
        n_i = column(nj[r][0:1, :])
        c_i = column(cl[r][0:1, :])
        n_j, c_j, self_id = [], [], []
        for k in range(K):
            t = tile_of(r, k)
            n_j.append(nj[t][0:1, :])
            c_j.append(jnp.where(k < cnt[r], cl[t][0:1, :], -1.0))
            self_id.append(jnp.where(t == r, rowid, -1))
        for b in range(TILE // RB):
            rs = slice(b * RB, (b + 1) * RB)
            dist = []
            for k in range(K):
                dot = gram[j, rs, k * TILE:(k + 1) * TILE]
                t = (n_i[rs] + n_j[k]) - 2.0 * dot
                ok = (c_i[rs] == c_j[k]) & (self_id[k][rs] != lane)
                dist.append(jnp.where(ok, t, FAR))
            low = jnp.minimum(jnp.minimum(dist[0], dist[1]), jnp.minimum(dist[2], dist[3]))
            near = jnp.min(low, axis=1, keepdims=True)
            w = [jnp.exp((near - t) * (1.0 / kernel_width)) for t in dist]
            total = jnp.sum((w[0] + w[1]) + (w[2] + w[3]), axis=1, keepdims=True)
            inv = 1.0 / total
            for k in range(K):
                aff[j, rs, k * TILE:(k + 1) * TILE] = (w[k] * inv).astype(jnp.bfloat16)

    def spread(j, labels):
        r = 2 * j + a
        acc = None
        for k in range(K):
            part = jnp.dot(aff[j, :, k * TILE:(k + 1) * TILE], labels[tile_of(r, k)],
                           preferred_element_type=jnp.float32)
            acc = part if acc is None else acc + part
        seeds = l0[r].astype(jnp.float32)
        return (spread_weight * acc + (1.0 - spread_weight) * seeds).astype(jnp.bfloat16)

    @pl.when(is_centre)
    def _():
        l0[g] = sd[...]
        for t in range(8):
            cl[t] = jnp.broadcast_to(wide(clu, t).astype(jnp.float32), (8, TILE))

        nb[0, a, 0] = own_n[...]
        @pl.when(even)
        def _():
            for q in range(FIRST):
                arrived(relay.at[rows(q)], rrl.at[q])
                from_relay(q).start()

        for q in [q for q in ORDER if q >= FIRST]:
            arrived(relay.at[rows(q)], rrl.at[q])
            from_relay(q).start()
        for q in range(CH):
            for d in (1, 3):
                arrived(x0.at[0, rows(0)], rx.at[d, q])
                fwd_x(d, q).start()

        @pl.when(has_next)
        def _():
            for d in range(4):
                arrived(x0.at[0, pl.ds(8, SPILL)], rsp.at[d])
                fwd_sp(d).start()
            arrived(cs, rcs.at[0])

        for q in range(CH):
            for d in (0, 1, 3):
                arrived(x0.at[0, rows(0)], fx.at[d, q])

        @pl.when(has_next)
        def _():
            for d in range(4):
                arrived(x0.at[0, pl.ds(8, SPILL)], fsp.at[d])

        for t in range(2):
            cl[8 + t] = jnp.broadcast_to(wide(cs, t).astype(jnp.float32), (8, TILE))

        def near(j, carry):
            products(j, (0, 1, 3), False)
            return carry

        lax.fori_loop(0, 4, near, 0)
        for q in ORDER:
            arrived(x0.at[0, rows(0)], rx.at[2, q])
            fwd_x(2, q).start()
        for d in (1, 2, 3):
            arrived(own_n, rn.at[d])
            fwd_norm(d).start()

        @pl.when(has_next)
        def _():
            for d in range(4):
                arrived(own_n, rns.at[d])
                fwd_spill_norm(d).start()

        for q in range(CH):
            arrived(x0.at[0, rows(0)], fx.at[2, q])
        for d in range(4):
            arrived(own_n, fn.at[d])

        @pl.when(has_next)
        def _():
            for d in range(4):
                arrived(own_n, fns.at[d])

        for part, tiles in ((0, 8), (1, SPILL)):
            total = nb[0, 0, part]
            for d, b in ((0, 1), (1, 0), (1, 1), (2, 0), (2, 1), (3, 0), (3, 1)):
                total += nb[d, b, part]
            for t in range(tiles):
                nj[8 * part + t] = jnp.broadcast_to(total[t:t + 1, :], (8, TILE))

        def affinity(j, carry):
            products(j, (2,), True)
            softmax(j)
            return carry

        def first_step(j, carry):
            l1[2 * j + a] = spread(j, l0)
            send_l1(j).start()

            @pl.when((j == 0) & has_prev)
            def _():
                spill_l1().start()

            return carry

        lax.fori_loop(0, EARLY, affinity, 0)
        for d in (1, 3, 2):
            arrived(l0.at[0], rsd.at[d])
            fwd_seed(d).start()

        @pl.when(has_next)
        def _():
            arrived(l0.at[0], rsd.at[4])
            fwd_seed(4).start()

        for d in range(4):
            arrived(l0.at[0], fsd.at[d])

        @pl.when(has_next)
        def _():
            arrived(l0.at[0], fsd.at[4])

        lax.fori_loop(0, EARLY, first_step, 0)

        def rest(j, carry):
            affinity(j, 0)
            return first_step(j, carry)

        lax.fori_loop(EARLY, 4, rest, 0)

        @pl.when(has_next)
        def _():
            arrived(l1.at[0], rl1s.at[0])
            fwd_l1().start()

        for j in range(4):
            arrived(l1.at[0], rl1.at[j])

        @pl.when(has_next)
        def _():
            arrived(l1.at[0], rl1s.at[1])

        for d in (1, 2, 3, 0):
            j = (c + d) % 4
            res[j] = spread(j, l1)
            if d == 0:
                own_result().start()
            else:
                result(d).start()

        for j in range(4):
            send_l1(j).wait_send()
        own_result().wait()
        for d in (1, 2, 3):
            result(d).wait_send()
            fwd_norm(d).wait_send()
        norm_to_partner().wait_send()
        own_l().wait_send()
        for q in range(CH):
            own_x(q).wait_send()
            for d in (1, 2, 3):
                fwd_x(d, q).wait_send()
        for d in (1, 2, 3):
            fwd_seed(d).wait_send()
        for q in range(FIRST, CH):
            from_relay(q).wait_send()

        @pl.when(even)
        def _():
            for q in range(FIRST):
                from_relay(q).wait_send()

        @pl.when(has_next)
        def _():
            for d in range(4):
                fwd_sp(d).wait_send()
                fwd_spill_norm(d).wait_send()
            fwd_seed(4).wait_send()
            fwd_l1().wait_send()

        @pl.when(has_prev)
        def _():
            spill_l1().wait_send()

    @pl.when(has_prev)
    def _():
        spill_norm().wait_send()

    for d in range(4):
        @pl.when(has_prev & (relp == d))
        def _(d=d):
            spill_x(d).wait_send()

    @pl.when(has_prev & (h == 0))
    def _():
        spill_clu().wait_send()
        spill_seed().wait_send()

    for d in (1, 3):
        @pl.when(rel == d)
        def _(d=d):
            own_seed(d).wait_send()

    @pl.when(rel == 2)
    def _():
        own_seed(2).wait_send()

    @pl.when(jnp.logical_not(is_centre))
    def _():
        norm_to_centre().wait_send()
        arrived(out, ro.at[0])


def local(embeddings, clusters, blocks, counts, seed_mask, prior):
    bf16, f32, i32 = jnp.bfloat16, jnp.float32, jnp.int32
    anyw = pl.BlockSpec(memory_space=pl.ANY)
    hbm = pl.BlockSpec(memory_space=pltpu.HBM)
    V, D = pltpu.VMEM, pltpu.SemaphoreType.DMA
    x = V((2, 10, TILE, 128), bf16)
    return pl.pallas_call(
        kernel,
        out_shape=jax.ShapeDtypeStruct((TILE, TILE), bf16),
        in_specs=[hbm] * 6,
        out_specs=anyw,
        scratch_shapes=[
            x, x, x, x,
            V((8, TILE, 128), bf16),
            V((TILE, TILE), bf16),
            V((TILE, TILE), bf16),
            V((8, 128), i32),
            V((10, TILE, TILE), bf16),
            V((10, TILE, TILE), bf16),
            V((4, TILE, K * TILE), f32),
            V((4, TILE, K * TILE), bf16),
            V((10, 8, TILE), f32),
            V((10, 8, TILE), f32),
            V((4, TILE, TILE), bf16),
            V((8, TILE), f32),
            V((4, 2, 2, 8, TILE), f32),
            V((16, 128), i32), pltpu.SMEM((4, 8), i32), pltpu.SMEM((8,), i32), V((2, 128), i32),
            D((6,)), D((4, CH)), D((4, CH)), D((4,)), D((4,)), D((5,)), D((5,)), D((1,)), D((CH,)),
            D((4,)), D((2,)), D((1,)),
            D((4,)), D((4,)), D((4,)), D((4,)), D((2,)), D((4,)), D((4,)),
            D((CH,)), D((1,)), D((2,)), D((1,)), D((CH,)), D((4, CH)), D((4,)), D((5,)), D((4,)), D((2,)), D((4,)),
        ],
        compiler_params=pltpu.CompilerParams(
            collective_id=0, has_side_effects=True, vmem_limit_bytes=60 * 1024 * 1024),
        name="spread",
    )(embeddings.reshape(8, TILE, 128), clusters.reshape(16, 128), blocks.T, counts,
      seed_mask.reshape(2, 128), prior)


def solution(mesh):
    in_specs = (
        P("shard", "grp"),
        P("shard"),
        P("shard", None),
        P("shard"),
        P(("shard", "grp")),
        P(("shard", "grp"), None),
    )
    out_specs = P(("shard", "grp"), None)
    return jax.shard_map(local, mesh=mesh, in_specs=in_specs, out_specs=out_specs, check_vma=False)
```
